512 devices in a mesh: ctx: 32 (over y, x_lo, core), head: 16 (over z, x_hi).
Axes of the slice: x: 4 (x_hi: 2, x_lo: 2; x = x_hi * 2 + x_lo), y: 8, z: 8, core: 2. Of those that a mesh axis runs over, the one named last changes fastest.
Arguments:
- hidden: bfloat16 [2, 4096, 7168], P(None, 'ctx', 'head'), may hold values from -6 to 6
- queries: bfloat16 [2, 4096, 12288], P(None, 'ctx', 'head'), may hold values from -260 to 260
- w_dkv: bfloat16 [7168, 576], P('head'), may hold values from -0.0625 to 0.0625
- kv_gain: float32 [512], replicated, may hold values from 0.1 to 1.9
- w_key: bfloat16 [64, 512, 128], P('head'), may hold values from -0.25 to 0.25
- w_val: bfloat16 [64, 512, 128], P('head'), may hold values from -0.25 to 0.25
- doc_lengths: int32 [16], replicated, may hold values from 1 to 1536, 8192 in all
Outputs:
- attended: bfloat16 [2, 4096, 8192], P(None, 'ctx', 'head')
The draws below stay inside these ranges and needn't reach their ends.
Inputs may be any that keep to these rules, and one draw needn't show every extreme that they name: `doc_lengths`: lengths sum to 8192; the longest is exactly 1536.
All inputs are finite; a program needn't handle non-finite values.
Results may differ from the reference program's by a relative error of at most 0.02.
The reference program's roundings to bfloat16 on the way count: a program that leaves them out, or rounds other values in their place, can miss the bound.
Values may be sent and summed in bfloat16 or wider, within the bound.
A program may use at most 64 MiB of HBM per device.

```python
import math
import jax
import jax.numpy as jnp
import numpy as np
from jax import lax

D = 7168
HEADS = 64
LATENT = 512
ROPE = 64
NOPE = 128
VDIM = 128
WINDOW = 1024
HALF = 128
STEPS = 8
HALF_SEQ = 4096
SEQ = 8192
NDOCS = 16
DOC_MOST = 1536
N_CTX = 32


def draw_queries(key, part):
    shape = (2, HALF_SEQ, HEADS * (NOPE + ROPE))
    return jnp.clip(jax.random.normal(key, shape, jnp.float32), -6.0, 6.0).astype(jnp.bfloat16)


def level_of(key, extent, pieces, least, high):
    loudness = 1.0
    for position, shards_of in pieces:
        heights = jax.random.uniform(jax.random.fold_in(jax.random.fold_in(key, 6), position), (shards_of,), jnp.float32, least / len(pieces), high / len(pieces))
        loudness = loudness * jnp.repeat(jnp.exp(heights), extent[position] // shards_of).reshape((-1,) + (1,) * (len(extent) - 1 - position))
    return loudness


def length_profile(count, total, bound, lean):
    weights = [(1 << 20) // math.isqrt(grade ** lean) + 1 for grade in range(2, count + 1)]
    surplus, given = total - bound - (count - 1), [1] * (count - 1)
    while surplus > 0:
        movable = [i for i in range(count - 1) if given[i] < bound]
        pool, remaining = sum([weights[i] for i in movable]), surplus
        for i in movable:
            addition = min(bound - given[i], max(1, remaining * weights[i] // pool), surplus)
            given[i] = given[i] + addition
            surplus = surplus - addition
    return np.array([bound] + given)


def ragged(stream_key, number_of, total, reach, skew):
    if number_of == 2:
        one = jax.random.randint(stream_key, (), max(1, total - reach), min(reach, total - 1) + 1)
        return jnp.stack([one, total - one])
    sizes = jnp.asarray(length_profile(number_of, total, reach, skew), jnp.int32)
    twos = (number_of - 1) // 2
    donor, taker = sizes[1:1 + 2 * twos:2], sizes[2:2 + 2 * twos:2]
    room = jnp.minimum(donor - 1, reach - taker)
    shifted = jax.random.randint(jax.random.fold_in(stream_key, 1), (twos,), 0, 1 << 20) % (room + 1)
    sizes = sizes.at[1:1 + 2 * twos:2].set(donor - shifted).at[2:2 + 2 * twos:2].set(taker + shifted)
    return sizes[jax.random.permutation(jax.random.fold_in(stream_key, 2), number_of)]


def bell_draw(stream_key, shape, scale, reach, cuts=(), held_as=jnp.bfloat16):
    result = jax.random.normal(stream_key, shape, jnp.float32) * scale
    if len(cuts) > 0:
        result = level_of(stream_key, shape, cuts, -0.22, 0.18) * result
    return jnp.clip(result, min=-reach, max=reach).astype(held_as)


def setup_inputs(seed: int = 0) -> dict:
    streams_of = jax.random.split(jax.random.key(seed), 8)
    return {
        "hidden": bell_draw(streams_of[0], (2, HALF_SEQ, D), 1.0, 6.0, ((1, 32), (2, 16))),
        "queries": draw_queries(jax.random.fold_in(streams_of[7], 71), 0),
        "w_dkv": bell_draw(streams_of[2], (D, LATENT + ROPE), D ** -0.5, 0.0625, ((0, 16),)),
        "kv_gain": jnp.clip(1.0 + 0.18 * jax.random.normal(streams_of[3], (LATENT,), jnp.float32), 0.1, 1.9),
        "w_key": bell_draw(streams_of[4], (HEADS, LATENT, NOPE), LATENT ** -0.5, 0.25, ((0, 16),)),
        "w_val": bell_draw(streams_of[5], (HEADS, LATENT, VDIM), LATENT ** -0.5, 0.25, ((0, 16),)),
        "doc_lengths": ragged(streams_of[6], NDOCS, SEQ, DOC_MOST, 1).astype(jnp.int32),
    }


def unfold(folded):
    tail = folded[1].reshape((N_CTX, HALF) + folded.shape[2:])[::-1].reshape(folded.shape[1:])
    return jnp.concatenate([folded[0], tail], axis=0)

def fold_back(sequence):
    leading = sequence[:HALF_SEQ]
    tail = sequence[HALF_SEQ:].reshape((N_CTX, HALF) + sequence.shape[1:])[::-1].reshape((HALF_SEQ,) + sequence.shape[1:])
    return jnp.stack([leading, tail])

def rotate(rope_part, positions):
    half_rope = ROPE // 2
    frequency = 10000.0 ** (-jnp.arange(half_rope, dtype=jnp.float32) / half_rope)
    angles = positions.astype(jnp.float32)[:, None] * frequency[None, :]
    cosine = jnp.cos(angles)
    sine_part = jnp.sin(angles)
    front_half = rope_part[:, :half_rope]
    back_half = rope_part[:, half_rope:]
    return jnp.concatenate([front_half * cosine - back_half * sine_part, back_half * cosine + front_half * sine_part], 1)

def finish_latent(latent, positions, kv_gain):
    compressed = latent[:, :LATENT]
    variance = lax.optimization_barrier(jnp.mean(compressed * compressed, axis=1, keepdims=True))
    normed = compressed * lax.rsqrt(variance + 1e-06) * kv_gain[None, :]
    rotated = rotate(latent[:, LATENT:], positions)
    return jnp.concatenate([normed, rotated], 1).astype(jnp.bfloat16)

def document_of(positions, doc_lengths):
    bounds = jnp.cumsum(doc_lengths, dtype=jnp.int32)
    return lax.optimization_barrier(jnp.sum((bounds[None, :] <= positions[:, None]).astype(jnp.int32), axis=1, dtype=jnp.int32))

def reference(hidden, queries, w_dkv, kv_gain, w_key, w_val, doc_lengths):
    seq_hidden = unfold(hidden)
    positions = jnp.arange(SEQ, dtype=jnp.int32)
    latent = jnp.dot(seq_hidden, w_dkv, preferred_element_type=jnp.float32)
    keys_all = finish_latent(latent, positions, kv_gain)
    documents = document_of(positions, doc_lengths)
    padded = jnp.concatenate([jnp.zeros((STEPS * HALF, LATENT + ROPE), jnp.bfloat16), keys_all], 0)
    doc_padded = jnp.concatenate([jnp.full((STEPS * HALF,), -1, jnp.int32), documents], 0)
    seq_queries = unfold(queries).reshape(2 * N_CTX, HALF, HEADS, NOPE + ROPE)
    score_scale = (NOPE + ROPE) ** (-0.5)

    def block_out(block_index):
        block_rows = lax.dynamic_index_in_dim(seq_queries, block_index, 0, keepdims=False)
        query_pos = block_index * HALF + jnp.arange(HALF, dtype=jnp.int32)
        absorbed = jnp.einsum('qhn,hln->hql', block_rows[..., :NOPE].astype(jnp.float32), w_key.astype(jnp.float32)).astype(jnp.bfloat16)
        query_full = jnp.concatenate([absorbed, jnp.transpose(block_rows[..., NOPE:], (1, 0, 2))], 2)
        start = (block_index * HALF).astype(jnp.int32)
        block_keys = lax.dynamic_slice_in_dim(padded, start, (STEPS + 1) * HALF, 0)
        key_doc = lax.dynamic_slice_in_dim(doc_padded, start, (STEPS + 1) * HALF, 0)
        key_pos = (block_index - STEPS) * HALF + jnp.arange((STEPS + 1) * HALF, dtype=jnp.int32)
        query_doc = lax.dynamic_slice_in_dim(documents, start, HALF, 0)
        visible = (key_pos[None, :] <= query_pos[:, None]) & (query_pos[:, None] - key_pos[None, :] < WINDOW) & (key_doc[None, :] == query_doc[:, None])
        scores = jnp.einsum('hql,kl->hqk', query_full.astype(jnp.float32), block_keys.astype(jnp.float32)) * score_scale
        masked = jnp.where(visible[None], scores, -jnp.inf)
        row_max = lax.optimization_barrier(jnp.max(masked, axis=2, keepdims=True))
        weights = jnp.exp(masked - row_max).astype(jnp.bfloat16)
        denominator = lax.optimization_barrier(jnp.sum(weights.astype(jnp.float32), axis=2, keepdims=True))
        numerator = jnp.einsum('hqk,kl->hql', weights.astype(jnp.float32), block_keys[:, :LATENT].astype(jnp.float32))
        mixed = (numerator / denominator).astype(jnp.bfloat16)
        values = jnp.einsum('hql,hlv->qhv', mixed.astype(jnp.float32), w_val.astype(jnp.float32)).astype(jnp.bfloat16)
        return values.reshape(HALF, HEADS * VDIM)
    results = lax.map(block_out, jnp.arange(2 * N_CTX, dtype=jnp.int32))
    return fold_back(results.reshape(SEQ, HEADS * VDIM))
```

```python
import functools

import jax
import jax.numpy as jnp
from jax import lax
from jax.experimental import pallas as pl
from jax.experimental.pallas import tpu as pltpu
from jax.sharding import PartitionSpec as P

LATENT = 512
ROPE = 64
NOPE = 128
VDIM = 128
KEY = LATENT + ROPE
WINDOW = 1024
SPAN = 9
BLOCK = 128
ROWS = 16
NEG = -1e30
MESH = pl.DeviceIdType.MESH

OFFSETS = [(dz, dx) for dz in (4, 3, -3, 2, -2, 1, -1, 0) for dx in (0, 1) if (dz, dx) != (0, 0)]
PEERS = len(OFFSETS)


def body(
    hidden_hbm, queries_hbm, w_dkv_hbm, gain_ref, w_key_hbm, w_val_hbm, docs_ref, trig_ref,
    out_ref,
    hidden_v, queries_v, w_dkv_v, w_key_v, w_val_v, part, arrived, keys, qfull, scores, rowmax,
    lower, probs,
    load_sem, rs_send, rs_recv, ag_send, ag_recv, win_send, win_recv,
):
    ctx = lax.axis_index("ctx")
    head = lax.axis_index("head")
    core = ctx % 2
    x_lo = (ctx // 2) % 2
    y = ctx // 4
    col = ctx % 4
    z = head // 2
    x_hi = head % 2
    heads = w_key_v.shape[0]

    def head_peer(dz, dx):
        return ((z + dz + 8) % 8) * 2 + (x_hi + dx) % 2

    same = (x_lo + core + 1) % 2
    down_head = z * 2 + (x_hi + same) % 2
    up_head = z * 2 + (x_hi + 1 - same) % 2
    across_ctx = 4 * y + 2 * (1 - x_lo) + core
    mate_ctx = 4 * y + 2 * x_lo + 1 - core
    mirror_ctx = 4 * y + 3 - col
    last = y // 7
    next_ctx = (1 - last) * (ctx + 4) + last * mirror_ctx

    barrier = pltpu.get_barrier_semaphore()

    def greet(to_ctx, to_head):
        pl.semaphore_signal(barrier, inc=1, device_id=(to_ctx, to_head), device_id_type=MESH)

    for dz, dx in OFFSETS:
        greet(ctx, head_peer(dz, dx))
    greet((ctx + 4) % 32, head)
    greet((ctx + 28) % 32, head)
    greet(mirror_ctx, head)
    greet(mate_ctx, head)
    greet(across_ctx, down_head)
    greet(across_ctx, up_head)

    loads = [
        pltpu.make_async_copy(source, target, load_sem.at[i])
        for i, (source, target) in enumerate(
            [
                (hidden_hbm, hidden_v),
                (w_dkv_hbm, w_dkv_v),
                (queries_hbm, queries_v),
                (w_key_hbm, w_key_v),
                (w_val_hbm, w_val_v),
            ]
        )
    ]
    for load in loads:
        load.start()
    loads[0].wait()
    loads[1].wait()
    for half in range(2):
        part[half * BLOCK : (half + 1) * BLOCK, :] = jnp.dot(
            hidden_v[half], w_dkv_v[...], preferred_element_type=jnp.float32
        )

    pl.semaphore_wait(barrier, PEERS + 6)

    rs = []
    for i, (dz, dx) in enumerate(OFFSETS):
        peer = head_peer(dz, dx)
        copy = pltpu.make_async_remote_copy(
            src_ref=part.at[pl.ds(pl.multiple_of(peer * ROWS, ROWS), ROWS), :],
            dst_ref=arrived.at[i],
            send_sem=rs_send.at[i],
            recv_sem=rs_recv.at[i],
            device_id=(ctx, peer),
            device_id_type=MESH,
        )
        copy.start()
        rs.append(copy)

    row = lax.broadcasted_iota(jnp.int32, (BLOCK, BLOCK), 0)
    lane = lax.broadcasted_iota(jnp.int32, (BLOCK, BLOCK), 1)
    for half in range(2):
        query_block = ctx if half == 0 else 63 - ctx
        position = query_block * BLOCK + row
        start = jnp.zeros((BLOCK, BLOCK), jnp.int32)
        bound = jnp.int32(0)
        for i in range(docs_ref.shape[0]):
            bound = bound + docs_ref[i]
            start = jnp.maximum(start, jnp.where(bound <= position, bound, 0))
        lower[half] = jnp.maximum(start - (query_block - (SPAN - 1)) * BLOCK, row + 1)

    loads[2].wait()
    loads[3].wait()
    for half in range(2):
        for n in range(heads):
            at = n * (NOPE + ROPE)
            rows = slice(n * BLOCK, (n + 1) * BLOCK)
            qfull[half, rows, :LATENT] = lax.dot_general(
                queries_v[half, :, at : at + NOPE],
                w_key_v[n],
                (((1,), (1,)), ((), ())),
                preferred_element_type=jnp.float32,
            ).astype(jnp.bfloat16)
            qfull[half, rows, LATENT:] = queries_v[half, :, at + NOPE : at + NOPE + ROPE]

    @pl.when(y == 0)
    def _():
        keys[0, 0] = jnp.zeros((BLOCK, KEY), jnp.bfloat16)
        keys[0, 4] = jnp.zeros((BLOCK, KEY), jnp.bfloat16)

    for copy in reversed(rs):
        copy.wait_recv()
    latent = part[pl.ds(pl.multiple_of(head * ROWS, ROWS), ROWS), :]
    for i in range(PEERS):
        latent = latent + arrived[i]
    compressed = latent[:, :LATENT]
    variance = jnp.mean(compressed * compressed, axis=1, keepdims=True)
    normed = compressed * lax.rsqrt(variance + 1e-06) * gain_ref[...]
    front, back = latent[:, LATENT : LATENT + ROPE // 2], latent[:, LATENT + ROPE // 2 :]
    cosine, sine = trig_ref[0], trig_ref[1]
    rotated = jnp.concatenate([front * cosine - back * sine, back * cosine + front * sine], 1)

    def piece(of_head):
        return keys.at[of_head // 8, 8, pl.ds(pl.multiple_of(of_head % 8 * ROWS, ROWS), ROWS), :]

    keys[head // 8, 8, pl.ds(pl.multiple_of(head % 8 * ROWS, ROWS), ROWS), :] = jnp.concatenate(
        [normed, rotated], 1
    ).astype(jnp.bfloat16)

    ag = []
    for i, (dz, dx) in enumerate(OFFSETS):
        copy = pltpu.make_async_remote_copy(
            src_ref=piece(head),
            dst_ref=piece(head),
            send_sem=ag_send.at[i],
            recv_sem=ag_recv.at[i],
            device_id=(ctx, head_peer(dz, dx)),
            device_id_type=MESH,
        )
        copy.start()
        ag.append(copy)
    for i, (dz, dx) in reversed(list(enumerate(OFFSETS))):
        come = piece(head_peer(-dz, dx))
        pltpu.make_async_remote_copy(
            src_ref=come,
            dst_ref=come,
            send_sem=ag_send.at[i],
            recv_sem=ag_recv.at[i],
            device_id=(ctx, head_peer(-dz, dx)),
            device_id_type=MESH,
        ).wait_recv()

    sent = []

    def send(condition, half, index, to_half, to_index, to_ctx, to_head):
        copy = pltpu.make_async_remote_copy(
            src_ref=keys.at[half, index],
            dst_ref=keys.at[to_half, to_index],
            send_sem=win_send.at[len(sent)],
            recv_sem=win_recv.at[to_half, to_index],
            device_id=(to_ctx, to_head),
            device_id_type=MESH,
        )
        sent.append((condition, copy))
        if condition is None:
            copy.start()
        else:
            pl.when(condition)(copy.start)

    def take(half, index):
        pltpu.make_async_remote_copy(
            src_ref=keys.at[half, index],
            dst_ref=keys.at[half, index],
            send_sem=win_send.at[0],
            recv_sem=win_recv.at[half, index],
            device_id=(ctx, head),
            device_id_type=MESH,
        ).wait_recv()

    def score(half, index):
        raw = lax.dot_general(
            qfull[half], keys[half, index], (((1,), (1,)), ((), ())), preferred_element_type=jnp.float32
        )
        seen = index * BLOCK + lane >= lower[half]
        if index == SPAN - 1:
            seen = seen & (lane <= row)
        masked = jnp.where(seen[None], raw.reshape(heads, BLOCK, BLOCK), NEG).reshape(heads * BLOCK, BLOCK)
        scores[half, index] = masked
        if index == SPAN - 1:
            rowmax[half] = masked
        else:
            rowmax[half] = jnp.maximum(rowmax[half], masked)

    first = y == 0
    onward = y > 0
    send(None, 0, 8, last, 4, next_ctx, head)
    send(onward, 1, 8, 1, 4, ctx - 4, head)
    send(x_lo == 0, 0, 8, 0, 6, across_ctx, down_head)
    send(x_lo == 1, 1, 8, 1, 6, across_ctx, down_head)
    send(core == 0, 0, 8, 0, 7, mate_ctx, head)
    send(core == 1, 1, 8, 1, 7, mate_ctx, head)
    score(0, 8)
    score(1, 8)

    pl.when(onward)(functools.partial(take, 0, 4))
    send(None, 0, 4, last, 0, next_ctx, head)
    send(None, 0, 4, 0, 2 + 4 * x_lo, across_ctx, down_head)
    send(None, 0, 4, 0, 3 + 2 * core, mate_ctx, head)
    take(1, 4)
    send(onward, 1, 4, 1, 0, ctx - 4, head)
    send(None, 1, 4, 1, 6 - 4 * x_lo, across_ctx, down_head)
    send(None, 1, 4, 1, 5 - 2 * core, mate_ctx, head)
    score(0, 4)
    score(1, 4)

    for half in range(2):
        take(half, 6)
        send(None, half, 6, half, 5 + 2 * core if half == 0 else 7 - 2 * core, mate_ctx, head)
    score(0, 6)
    score(1, 6)

    pl.when(onward)(functools.partial(take, 0, 0))
    send(x_lo == 1, 0, 0, 0, 2, across_ctx, down_head)
    send(core == 1, 0, 0, 0, 1, mate_ctx, head)
    take(1, 0)
    send(x_lo == 0, 1, 0, 1, 2, across_ctx, down_head)
    send(core == 0, 1, 0, 1, 1, mate_ctx, head)
    score(0, 0)
    score(1, 0)

    for half in range(2):
        take(half, 2)
        send(None, half, 2, half, 1 + 2 * core if half == 0 else 3 - 2 * core, mate_ctx, head)
    score(0, 2)
    score(1, 2)
    for index in (7, 5, 3, 1):
        for half in range(2):
            take(half, index)
            score(half, index)

    loads[4].wait()
    to_log2 = (NOPE + ROPE) ** -0.5 * 1.4426950408889634
    for half in range(2):
        top = jnp.max(rowmax[half], axis=1, keepdims=True)
        total = jnp.zeros((heads * BLOCK, BLOCK), jnp.float32)
        for index in range(SPAN):
            weight = jnp.exp2((scores[half, index] - top) * to_log2).astype(jnp.bfloat16)
            probs[:, index * BLOCK : (index + 1) * BLOCK] = weight
            total = total + weight.astype(jnp.float32)
        denominator = jnp.sum(total, axis=1, keepdims=True)
        values = keys[half].reshape(SPAN * BLOCK, KEY)[:, :LATENT]
        numerator = jnp.dot(probs[...], values, preferred_element_type=jnp.float32)
        mixed = (numerator * (1.0 / denominator)).astype(jnp.bfloat16)
        for n in range(heads):
            out_ref[half, :, n * VDIM : (n + 1) * VDIM] = jnp.dot(
                mixed[n * BLOCK : (n + 1) * BLOCK], w_val_v[n], preferred_element_type=jnp.float32
            ).astype(jnp.bfloat16)

    for copy in rs + ag:
        copy.wait_send()
    for condition, copy in sent:
        if condition is None:
            copy.wait_send()
        else:
            pl.when(condition)(copy.wait_send)


def on_device(hidden, queries, w_dkv, kv_gain, w_key, w_val, doc_lengths):
    ctx = lax.axis_index("ctx")
    head = lax.axis_index("head")
    heads = w_key.shape[0]
    block = jnp.where(head < 8, ctx, 63 - ctx)
    positions = block * BLOCK + head % 8 * ROWS + jnp.arange(ROWS, dtype=jnp.int32)
    half_rope = ROPE // 2
    frequency = 10000.0 ** (-jnp.arange(half_rope, dtype=jnp.float32) / half_rope)
    angles = positions.astype(jnp.float32)[:, None] * frequency[None, :]
    trig = jnp.stack([jnp.cos(angles), jnp.sin(angles)])
    any_space = pl.BlockSpec(memory_space=pl.ANY)
    in_vmem = pl.BlockSpec(memory_space=pltpu.VMEM)
    bf16, f32 = jnp.bfloat16, jnp.float32
    dma = pltpu.SemaphoreType.DMA
    return pl.pallas_call(
        body,
        out_shape=jax.ShapeDtypeStruct((2, BLOCK, heads * VDIM), bf16),
        in_specs=[any_space, any_space, any_space, in_vmem, any_space, any_space,
                  pl.BlockSpec(memory_space=pltpu.SMEM), in_vmem],
        out_specs=in_vmem,
        scratch_shapes=[
            pltpu.VMEM(hidden.shape, bf16),
            pltpu.VMEM(queries.shape, bf16),
            pltpu.VMEM(w_dkv.shape, bf16),
            pltpu.VMEM(w_key.shape, bf16),
            pltpu.VMEM(w_val.shape, bf16),
            pltpu.VMEM((2 * BLOCK, KEY), f32),
            pltpu.VMEM((PEERS, ROWS, KEY), f32),
            pltpu.VMEM((2, SPAN, BLOCK, KEY), bf16),
            pltpu.VMEM((2, heads * BLOCK, KEY), bf16),
            pltpu.VMEM((2, SPAN, heads * BLOCK, BLOCK), f32),
            pltpu.VMEM((2, heads * BLOCK, BLOCK), f32),
            pltpu.VMEM((2, BLOCK, BLOCK), jnp.int32),
            pltpu.VMEM((heads * BLOCK, SPAN * BLOCK), bf16),
            dma((5,)), dma((PEERS,)), dma((PEERS,)), dma((PEERS,)), dma((PEERS,)),
            dma((24,)), dma((2, SPAN)),
        ],
        compiler_params=pltpu.CompilerParams(
            collective_id=0, has_side_effects=True, vmem_limit_bytes=60 * 1024 * 1024
        ),
    )(hidden, queries, w_dkv, kv_gain.reshape(1, LATENT), w_key, w_val, doc_lengths, trig)


def solution(mesh):
    in_specs = (
        P(None, "ctx", "head"),
        P(None, "ctx", "head"),
        P("head", None),
        P(),
        P("head", None, None),
        P("head", None, None),
        P(),
    )
    out_specs = P(None, "ctx", "head")
    return jax.shard_map(
        on_device, mesh=mesh, in_specs=in_specs, out_specs=out_specs, check_vma=False
    )
```

```python
import functools

import jax
import jax.numpy as jnp
import numpy as np
from jax import lax
from jax.experimental import pallas as pl
from jax.experimental.pallas import tpu as pltpu
from jax.sharding import PartitionSpec as P

LATENT = 512
ROPE = 64
NOPE = 128
VDIM = 128
KEY = LATENT + ROPE
WINDOW = 1024
SPAN = 9
BLOCK = 128
ROWS = 16
CHUNK = 64
PARTS = BLOCK // CHUNK
AHEAD = 4
BEHIND = 3
NEG = -1e30
MESH = pl.DeviceIdType.MESH

OFFSETS = [(dz, dx) for dz in (4, 3, -3, 2, -2, 1, -1, 0) for dx in (0, 1) if (dz, dx) != (0, 0)]
PEERS = len(OFFSETS)


def body(
    hidden_hbm, queries_hbm, w_dkv_hbm, gain_hbm, w_key_hbm, w_val_hbm, docs_hbm, turn_block_hbm, turn_row_hbm,
    out_ref,
    hidden_v, queries_v, w_dkv_v, gain_v, w_key_v, w_val_v, docs_s, turn_block_v, turn_row_v,
    part, forward, backward, crossed, keys, qfull, scores, rowmax, lower, probs,
    load_sem, fw_send, fw_recv, bw_send, bw_recv, cross_sem, ag_send, ag_recv, win_send, win_recv,
):
    ctx = lax.axis_index("ctx")
    head = lax.axis_index("head")
    core = ctx % 2
    x_lo = (ctx // 2) % 2
    y = ctx // 4
    col = ctx % 4
    z = head // 2
    x_hi = head % 2
    heads = w_key_v.shape[0]

    def head_peer(dz, dx):
        return ((z + dz + 8) % 8) * 2 + (x_hi + dx) % 2

    same = (x_lo + core + 1) % 2
    down_head = z * 2 + (x_hi + same) % 2
    up_head = z * 2 + (x_hi + 1 - same) % 2
    across_ctx = 4 * y + 2 * (1 - x_lo) + core
    mate_ctx = 4 * y + 2 * x_lo + 1 - core
    mirror_ctx = 4 * y + 3 - col
    last = y // 7
    next_ctx = (1 - last) * (ctx + 4) + last * mirror_ctx
    next_head = (1 - last) * head + last * down_head

    barrier = pltpu.get_barrier_semaphore()

    def greet(to_ctx, to_head):
        pl.semaphore_signal(barrier, inc=1, device_id=(to_ctx, to_head), device_id_type=MESH)

    greet(ctx, head_peer(1, 0))
    greet(ctx, head_peer(-1, 0))
    greet(ctx, head_peer(0, 1))
    greet(across_ctx, down_head)
    greet(across_ctx, up_head)
    greet((ctx + 4) % 32, head)
    greet((ctx + 28) % 32, head)
    greet(mirror_ctx, down_head)
    greet(mate_ctx, head)

    loads = [
        pltpu.make_async_copy(source, target, load_sem.at[i])
        for i, (source, target) in enumerate(
            [
                (hidden_hbm, hidden_v),
                (w_dkv_hbm, w_dkv_v),
                (queries_hbm, queries_v),
                (w_key_hbm, w_key_v),
                (w_val_hbm, w_val_v),
                (docs_hbm, docs_s),
                (gain_hbm, gain_v),
                (turn_block_hbm, turn_block_v),
                (turn_row_hbm, turn_row_v),
            ]
        )
    ]
    for load in loads:
        load.start()
    loads[0].wait()
    loads[1].wait()
    for half in range(2):
        part[half * BLOCK : (half + 1) * BLOCK, :] = lax.dot_general(
            hidden_v[half], w_dkv_v[...], (((0,), (0,)), ((), ())), preferred_element_type=jnp.float32
        )

    pl.semaphore_wait(barrier, 9)

    def rows_of(dz, dx):
        return pl.ds(pl.multiple_of(head_peer(dz, dx) * ROWS, ROWS), ROWS)

    def pass_on(step, dx, ahead):
        i = dx * AHEAD + step
        copy = pltpu.make_async_remote_copy(
            src_ref=part.at[rows_of(AHEAD - step if ahead else step - BEHIND, dx), :],
            dst_ref=(forward if ahead else backward).at[i],
            send_sem=(fw_send if ahead else bw_send).at[i],
            recv_sem=(fw_recv if ahead else bw_recv).at[i],
            device_id=(ctx, head_peer(1 if ahead else -1, 0)),
            device_id_type=MESH,
        )
        copy.start()
        return copy

    rs = {}
    for dx in (1, 0):
        rs[0, dx, True] = pass_on(0, dx, True)
        rs[0, dx, False] = pass_on(0, dx, False)

    def collect(step, dx, ahead):
        i = dx * AHEAD + step
        rs[step, dx, ahead].wait_recv()
        rows = rows_of(AHEAD - 1 - step if ahead else step + 1 - BEHIND, dx)
        part[rows, :] = part[rows, :] + (forward if ahead else backward)[i]

    row = lax.broadcasted_iota(jnp.int32, (BLOCK, BLOCK), 0)
    lane = lax.broadcasted_iota(jnp.int32, (BLOCK, BLOCK), 1)

    def bounds():
        loads[5].wait()
        for half in range(2):
            query_block = ctx if half == 0 else 63 - ctx
            position = query_block * BLOCK + row
            start = jnp.zeros((BLOCK, BLOCK), jnp.int32)
            bound = jnp.int32(0)
            for i in range(docs_s.shape[0]):
                bound = bound + docs_s[i]
                start = jnp.maximum(start, jnp.where(bound <= position, bound, 0))
            lower[half] = jnp.maximum(start - (query_block - (SPAN - 1)) * BLOCK, row + 1)

    def absorb(half):
        for n in range(heads):
            at = n * (NOPE + ROPE)
            rows = slice(n * BLOCK, (n + 1) * BLOCK)
            qfull[half, rows, :LATENT] = lax.dot_general(
                queries_v[half, :, at : at + NOPE],
                w_key_v[n],
                (((1,), (1,)), ((), ())),
                preferred_element_type=jnp.float32,
            ).astype(jnp.bfloat16)
            qfull[half, rows, LATENT:] = queries_v[half, :, at + NOPE : at + NOPE + ROPE]

    def fill(step):
        if step == 0:
            bounds()
        elif step == 1:
            loads[2].wait()
            loads[3].wait()
            absorb(0)
        else:
            absorb(1)

    @pl.when(y == 0)
    def _():
        keys[0, 0] = jnp.zeros((BLOCK, KEY), jnp.bfloat16)
        keys[0, 4] = jnp.zeros((BLOCK, KEY), jnp.bfloat16)

    for step in range(AHEAD - 1):
        fill(step)
        for dx in (1, 0):
            collect(step, dx, True)
            rs[step + 1, dx, True] = pass_on(step + 1, dx, True)
            if step < BEHIND - 1:
                collect(step, dx, False)
                rs[step + 1, dx, False] = pass_on(step + 1, dx, False)
    collect(BEHIND - 1, 1, False)
    collect(AHEAD - 1, 1, True)
    cross = pltpu.make_async_remote_copy(
        src_ref=part.at[rows_of(0, 1), :],
        dst_ref=crossed,
        send_sem=cross_sem.at[0],
        recv_sem=cross_sem.at[1],
        device_id=(ctx, head_peer(0, 1)),
        device_id_type=MESH,
    )
    cross.start()
    collect(BEHIND - 1, 0, False)
    collect(AHEAD - 1, 0, True)
    for i in (6, 7, 8):
        loads[i].wait()
    key_block = (1 - head // 8) * ctx + head // 8 * (63 - ctx)
    by_block = turn_block_v[pl.ds(key_block, 1), :]
    by_row = turn_row_v[pl.ds(pl.multiple_of(head % 8 * ROWS, ROWS), ROWS), :]
    quarter = ROPE // 2
    cos_a, sin_a = by_block[:, :quarter], by_block[:, quarter:]
    cos_b, sin_b = by_row[:, :quarter], by_row[:, quarter:]
    cosine = cos_a * cos_b - sin_a * sin_b
    sine = sin_a * cos_b + cos_a * sin_b

    cross.wait_recv()
    latent = part[rows_of(0, 0), :] + crossed[...]
    compressed = latent[:, :LATENT]
    variance = jnp.mean(compressed * compressed, axis=1, keepdims=True)
    normed = compressed * lax.rsqrt(variance + 1e-06) * gain_v[...]
    front, back = latent[:, LATENT : LATENT + quarter], latent[:, LATENT + quarter :]
    rotated = jnp.concatenate([front * cosine - back * sine, back * cosine + front * sine], 1)

    def piece(of_head):
        return keys.at[of_head // 8, 8, pl.ds(pl.multiple_of(of_head % 8 * ROWS, ROWS), ROWS), :]

    keys[head // 8, 8, pl.ds(pl.multiple_of(head % 8 * ROWS, ROWS), ROWS), :] = jnp.concatenate(
        [normed, rotated], 1
    ).astype(jnp.bfloat16)

    ag = []
    for i, (dz, dx) in enumerate(OFFSETS):
        copy = pltpu.make_async_remote_copy(
            src_ref=piece(head),
            dst_ref=piece(head),
            send_sem=ag_send.at[i],
            recv_sem=ag_recv.at[head],
            device_id=(ctx, head_peer(dz, dx)),
            device_id_type=MESH,
        )
        copy.start()
        ag.append(copy)

    def gathered(half, part_index):
        for i in range(CHUNK // ROWS):
            of_head = half * 8 + part_index * (CHUNK // ROWS) + i

            @pl.when(head != of_head)
            def _():
                pltpu.make_async_remote_copy(
                    src_ref=piece(of_head),
                    dst_ref=piece(of_head),
                    send_sem=ag_send.at[0],
                    recv_sem=ag_recv.at[of_head],
                    device_id=(ctx, head_peer(1, 0)),
                    device_id_type=MESH,
                ).wait_recv()

    sent = []

    def chunk(half, index, u):
        return keys.at[half, index, pl.ds(u * CHUNK, CHUNK), :]

    def send(condition, half, index, u, to_half, to_index, to_ctx, to_head):
        copy = pltpu.make_async_remote_copy(
            src_ref=chunk(half, index, u),
            dst_ref=chunk(to_half, to_index, u),
            send_sem=win_send.at[len(sent)],
            recv_sem=win_recv.at[to_half, to_index, u],
            device_id=(to_ctx, to_head),
            device_id_type=MESH,
        )
        sent.append((condition, copy))
        if condition is None:
            copy.start()
        else:
            pl.when(condition)(copy.start)

    def take(half, index, u):
        pltpu.make_async_remote_copy(
            src_ref=chunk(half, index, u),
            dst_ref=chunk(half, index, u),
            send_sem=win_send.at[0],
            recv_sem=win_recv.at[half, index, u],
            device_id=(mate_ctx, head),
            device_id_type=MESH,
        ).wait_recv()

    def score(half, index):
        raw = lax.dot_general(
            qfull[half], keys[half, index], (((1,), (1,)), ((), ())), preferred_element_type=jnp.float32
        )
        seen = index * BLOCK + lane >= lower[half]
        if index == SPAN - 1:
            seen = seen & (lane <= row)
        masked = jnp.where(seen[None], raw.reshape(heads, BLOCK, BLOCK), NEG).reshape(heads * BLOCK, BLOCK)
        scores[half, index] = masked
        if index == SPAN - 1:
            rowmax[half] = masked
        else:
            rowmax[half] = jnp.maximum(rowmax[half], masked)

    onward = y > 0
    for u in range(PARTS):
        gathered(0, u)
        send(None, 0, 8, u, last, 4, next_ctx, next_head)
        send(x_lo == 0, 0, 8, u, 0, 6, across_ctx, down_head)
        send(core == 0, 0, 8, u, 0, 7, mate_ctx, head)
    for u in range(PARTS):
        gathered(1, u)
        send(onward, 1, 8, u, 1, 4, ctx - 4, head)
        send(x_lo == 1, 1, 8, u, 1, 6, across_ctx, down_head)
        send(core == 1, 1, 8, u, 1, 7, mate_ctx, head)
    score(0, 8)
    score(1, 8)

    for u in range(PARTS):
        pl.when(onward)(functools.partial(take, 0, 4, u))
        send(None, 0, 4, u, last, 0, next_ctx, next_head)
        send(None, 0, 4, u, 0, 2 + 4 * x_lo, across_ctx, down_head)
        send(None, 0, 4, u, 0, 3 + 2 * core, mate_ctx, head)
        take(1, 4, u)
        send(onward, 1, 4, u, 1, 0, ctx - 4, head)
        send(None, 1, 4, u, 1, 6 - 4 * x_lo, across_ctx, down_head)
        send(None, 1, 4, u, 1, 5 - 2 * core, mate_ctx, head)
    score(0, 4)
    score(1, 4)

    for u in range(PARTS):
        for half in range(2):
            take(half, 6, u)
            send(None, half, 6, u, half, 5 + 2 * core if half == 0 else 7 - 2 * core, mate_ctx, head)
    score(0, 6)
    score(1, 6)

    for u in range(PARTS):
        pl.when(onward)(functools.partial(take, 0, 0, u))
        send(x_lo == 1, 0, 0, u, 0, 2, across_ctx, down_head)
        send(core == 1, 0, 0, u, 0, 1, mate_ctx, head)
        take(1, 0, u)
        send(x_lo == 0, 1, 0, u, 1, 2, across_ctx, down_head)
        send(core == 0, 1, 0, u, 1, 1, mate_ctx, head)
    score(0, 0)
    score(1, 0)

    for u in range(PARTS):
        for half in range(2):
            take(half, 2, u)
            send(None, half, 2, u, half, 1 + 2 * core if half == 0 else 3 - 2 * core, mate_ctx, head)
    score(0, 2)
    score(1, 2)
    for index in (7, 5, 3, 1):
        for half in range(2):
            for u in range(PARTS):
                take(half, index, u)
            score(half, index)

    loads[4].wait()
    to_log2 = (NOPE + ROPE) ** -0.5 * 1.4426950408889634
    for half in range(2):
        top = jnp.max(rowmax[half], axis=1, keepdims=True)
        total = jnp.zeros((heads * BLOCK, BLOCK), jnp.float32)
        for index in range(SPAN):
            weight = jnp.exp2((scores[half, index] - top) * to_log2).astype(jnp.bfloat16)
            probs[:, index * BLOCK : (index + 1) * BLOCK] = weight
            total = total + weight.astype(jnp.float32)
        denominator = jnp.sum(total, axis=1, keepdims=True)
        values = keys[half].reshape(SPAN * BLOCK, KEY)[:, :LATENT]
        numerator = jnp.dot(probs[...], values, preferred_element_type=jnp.float32)
        mixed = (numerator * (1.0 / denominator)).astype(jnp.bfloat16)
        for n in range(heads):
            out_ref[half, :, n * VDIM : (n + 1) * VDIM] = jnp.dot(
                mixed[n * BLOCK : (n + 1) * BLOCK], w_val_v[n], preferred_element_type=jnp.float32
            ).astype(jnp.bfloat16)

    for copy in [*rs.values(), cross, *ag]:
        copy.wait_send()
    for condition, copy in sent:
        if condition is None:
            copy.wait_send()
        else:
            pl.when(condition)(copy.wait_send)


def turns(positions):
    angles = positions[:, None] * 10000.0 ** (-np.arange(ROPE // 2) / (ROPE // 2))[None, :]
    return np.concatenate([np.cos(angles), np.sin(angles)], 1).astype(np.float32)


def on_device(hidden, queries, w_dkv, kv_gain, w_key, w_val, doc_lengths):
    heads = w_key.shape[0]
    hidden = jnp.swapaxes(hidden, 1, 2)
    turn_block = jnp.asarray(turns(np.arange(64) * BLOCK))
    turn_row = jnp.asarray(turns(np.arange(BLOCK)))
    any_space = pl.BlockSpec(memory_space=pl.ANY)
    in_vmem = pl.BlockSpec(memory_space=pltpu.VMEM)
    bf16, f32 = jnp.bfloat16, jnp.float32
    dma = pltpu.SemaphoreType.DMA
    return pl.pallas_call(
        body,
        out_shape=jax.ShapeDtypeStruct((2, BLOCK, heads * VDIM), bf16),
        in_specs=[any_space] * 9,
        out_specs=in_vmem,
        scratch_shapes=[
            pltpu.VMEM(hidden.shape, bf16),
            pltpu.VMEM(queries.shape, bf16),
            pltpu.VMEM(w_dkv.shape, bf16),
            pltpu.VMEM((1, LATENT), f32),
            pltpu.VMEM(w_key.shape, bf16),
            pltpu.VMEM(w_val.shape, bf16),
            pltpu.SMEM(doc_lengths.shape, jnp.int32),
            pltpu.VMEM(turn_block.shape, f32),
            pltpu.VMEM(turn_row.shape, f32),
            pltpu.VMEM((2 * BLOCK, KEY), f32),
            pltpu.VMEM((2 * AHEAD, ROWS, KEY), f32),
            pltpu.VMEM((2 * AHEAD, ROWS, KEY), f32),
            pltpu.VMEM((ROWS, KEY), f32),
            pltpu.VMEM((2, SPAN, BLOCK, KEY), bf16),
            pltpu.VMEM((2, heads * BLOCK, KEY), bf16),
            pltpu.VMEM((2, SPAN, heads * BLOCK, BLOCK), f32),
            pltpu.VMEM((2, heads * BLOCK, BLOCK), f32),
            pltpu.VMEM((2, BLOCK, BLOCK), jnp.int32),
            pltpu.VMEM((heads * BLOCK, SPAN * BLOCK), bf16),
            dma((9,)), dma((2 * AHEAD,)), dma((2 * AHEAD,)), dma((2 * AHEAD,)), dma((2 * AHEAD,)), dma((2,)),
            dma((PEERS,)), dma((PEERS + 1,)), dma((40,)), dma((2, SPAN, PARTS)),
        ],
        compiler_params=pltpu.CompilerParams(
            collective_id=0, has_side_effects=True, vmem_limit_bytes=60 * 1024 * 1024
        ),
    )(hidden, queries, w_dkv, kv_gain.reshape(1, LATENT), w_key, w_val, doc_lengths, turn_block, turn_row)


def solution(mesh):
    in_specs = (
        P(None, "ctx", "head"),
        P(None, "ctx", "head"),
        P("head", None),
        P(),
        P("head", None, None),
        P("head", None, None),
        P(),
    )
    out_specs = P(None, "ctx", "head")
    return jax.shard_map(
        on_device, mesh=mesh, in_specs=in_specs, out_specs=out_specs, check_vma=False
    )
```

```python
import functools

import jax
import jax.numpy as jnp
import numpy as np
from jax import lax
from jax.experimental import pallas as pl
from jax.experimental.pallas import tpu as pltpu
from jax.sharding import PartitionSpec as P

LATENT = 512
ROPE = 64
NOPE = 128
VDIM = 128
KEY = LATENT + ROPE
WINDOW = 1024
SPAN = 9
BLOCK = 128
ROWS = 16
CHUNK = 64
PARTS = BLOCK // CHUNK
REACH = 3
SLOT = {8: 0, 4: 1, 0: 2, 6: 3, 2: 4, 7: 5, 5: 6, 1: 7, 3: 8}
EARLY = 4
NEG = -1e30
MESH = pl.DeviceIdType.MESH

OFFSETS = [(dz, dx) for dz in (4, 3, -3, 2, -2, 1, -1, 0) for dx in (0, 1) if (dz, dx) != (0, 0)]
PEERS = len(OFFSETS)


def body(
    hidden_hbm, queries_hbm, w_dkv_hbm, gain_hbm, w_key_hbm, w_val_hbm, docs_hbm, turn_block_hbm, turn_row_hbm,
    out_ref,
    hidden_v, queries_v, w_dkv_v, gain_v, w_key_v, w_val_v, docs_s, turn_block_v, turn_row_v,
    part, forward, backward, opposite, crossed, keys, qfull, scores, rowmax, lower, probs, top_early, total_early, mixing,
    load_sem, fw_send, fw_recv, bw_send, bw_recv, op_send, op_recv, cross_sem, ag_send, ag_recv, win_send, win_recv,
):
    ctx = lax.axis_index("ctx")
    head = lax.axis_index("head")
    core = ctx % 2
    x_lo = (ctx // 2) % 2
    y = ctx // 4
    col = ctx % 4
    z = head // 2
    x_hi = head % 2
    heads = w_key_v.shape[0]

    def head_peer(dz, dx):
        return ((z + dz + 8) % 8) * 2 + (x_hi + dx) % 2

    same = (x_lo + core + 1) % 2
    down_head = z * 2 + (x_hi + same) % 2
    up_head = z * 2 + (x_hi + 1 - same) % 2
    across_ctx = 4 * y + 2 * (1 - x_lo) + core
    mate_ctx = 4 * y + 2 * x_lo + 1 - core
    mirror_ctx = 4 * y + 3 - col
    last = y // 7
    next_ctx = (1 - last) * (ctx + 4) + last * mirror_ctx
    next_head = (1 - last) * head + last * down_head

    barrier = pltpu.get_barrier_semaphore()

    def greet(to_ctx, to_head):
        pl.semaphore_signal(barrier, inc=1, device_id=(to_ctx, to_head), device_id_type=MESH)

    greet(ctx, head_peer(1, 0))
    greet(ctx, head_peer(-1, 0))
    greet(ctx, head_peer(4, 0))
    greet(ctx, head_peer(0, 1))
    greet(across_ctx, down_head)
    greet(across_ctx, up_head)
    greet((ctx + 4) % 32, head)
    greet((ctx + 28) % 32, head)
    greet(mirror_ctx, down_head)
    greet(mate_ctx, head)

    loads = [
        pltpu.make_async_copy(source, target, load_sem.at[i])
        for i, (source, target) in enumerate(
            [
                (hidden_hbm, hidden_v),
                (w_dkv_hbm, w_dkv_v),
                (queries_hbm, queries_v),
                (w_key_hbm, w_key_v),
                (w_val_hbm, w_val_v),
                (docs_hbm, docs_s),
                (gain_hbm, gain_v),
                (turn_block_hbm, turn_block_v),
                (turn_row_hbm, turn_row_v),
            ]
        )
    ]
    loads[0].start()
    loads[1].start()
    loads[0].wait()
    loads[1].wait()
    for load in loads[2:]:
        load.start()
    for half in range(2):
        part[half * BLOCK : (half + 1) * BLOCK, :] = lax.dot_general(
            hidden_v[half], w_dkv_v[...], (((0,), (0,)), ((), ())), preferred_element_type=jnp.float32
        )

    pl.semaphore_wait(barrier, 10)

    def rows_of(dz, dx):
        return pl.ds(pl.multiple_of(head_peer(dz, dx) * ROWS, ROWS), ROWS)

    def pass_on(step, dx, way):
        i = dx * REACH + step
        copy = pltpu.make_async_remote_copy(
            src_ref=part.at[rows_of(way * (REACH - step), dx), :],
            dst_ref=(forward if way == 1 else backward).at[i],
            send_sem=(fw_send if way == 1 else bw_send).at[i],
            recv_sem=(fw_recv if way == 1 else bw_recv).at[i],
            device_id=(ctx, head_peer(way, 0)),
            device_id_type=MESH,
        )
        copy.start()
        return copy

    rs = {}
    for dx in (1, 0):
        for way in (1, -1):
            rs[0, dx, way] = pass_on(0, dx, way)
    straight = []
    for dx in (1, 0):
        copy = pltpu.make_async_remote_copy(
            src_ref=part.at[rows_of(4, dx), :],
            dst_ref=opposite.at[dx],
            send_sem=op_send.at[dx],
            recv_sem=op_recv.at[dx],
            device_id=(ctx, head_peer(4, 0)),
            device_id_type=MESH,
        )
        copy.start()
        straight.append(copy)

    def collect(step, dx, way):
        i = dx * REACH + step
        rs[step, dx, way].wait_recv()
        rows = rows_of(way * (REACH - 1 - step), dx)
        part[rows, :] = part[rows, :] + (forward if way == 1 else backward)[i]

    def collect_all(dx):
        for way in (1, -1):
            rs[REACH - 1, dx, way].wait_recv()
        straight[1 - dx].wait_recv()
        i = dx * REACH + REACH - 1
        rows = rows_of(0, dx)
        part[rows, :] = part[rows, :] + forward[i] + (backward[i] + opposite[dx])

    row = lax.broadcasted_iota(jnp.int32, (BLOCK, BLOCK), 0)
    lane = lax.broadcasted_iota(jnp.int32, (BLOCK, BLOCK), 1)

    def bounds():
        loads[5].wait()
        for half in range(2):
            query_block = ctx if half == 0 else 63 - ctx
            position = query_block * BLOCK + row
            start = jnp.zeros((BLOCK, BLOCK), jnp.int32)
            bound = jnp.int32(0)
            for i in range(docs_s.shape[0]):
                bound = bound + docs_s[i]
                start = jnp.maximum(start, jnp.where(bound <= position, bound, 0))
            lower[half] = jnp.maximum(start - (query_block - (SPAN - 1)) * BLOCK, row + 1)

    def absorb(half):
        for n in range(heads):
            at = n * (NOPE + ROPE)
            rows = slice(n * BLOCK, (n + 1) * BLOCK)
            qfull[half, rows, :LATENT] = lax.dot_general(
                queries_v[half, :, at : at + NOPE],
                w_key_v[n],
                (((1,), (1,)), ((), ())),
                preferred_element_type=jnp.float32,
            ).astype(jnp.bfloat16)
            qfull[half, rows, LATENT:] = queries_v[half, :, at + NOPE : at + NOPE + ROPE]

    def fill(step):
        if step == 0:
            bounds()
        elif step == 1:
            loads[2].wait()
            loads[3].wait()
            absorb(0)
        else:
            absorb(1)

    @pl.when(y == 0)
    def _():
        keys[0, SLOT[0]] = jnp.zeros((BLOCK, KEY), jnp.bfloat16)
        keys[0, SLOT[4]] = jnp.zeros((BLOCK, KEY), jnp.bfloat16)

    for step in range(REACH - 1):
        fill(step)
        for dx in (1, 0):
            for way in (1, -1):
                collect(step, dx, way)
                rs[step + 1, dx, way] = pass_on(step + 1, dx, way)
    fill(REACH - 1)
    collect_all(1)
    cross = pltpu.make_async_remote_copy(
        src_ref=part.at[rows_of(0, 1), :],
        dst_ref=crossed,
        send_sem=cross_sem.at[0],
        recv_sem=cross_sem.at[1],
        device_id=(ctx, head_peer(0, 1)),
        device_id_type=MESH,
    )
    cross.start()
    collect_all(0)
    for i in (6, 7, 8):
        loads[i].wait()
    key_block = (1 - head // 8) * ctx + head // 8 * (63 - ctx)
    by_block = turn_block_v[pl.ds(key_block, 1), :]
    by_row = turn_row_v[pl.ds(pl.multiple_of(head % 8 * ROWS, ROWS), ROWS), :]
    quarter = ROPE // 2
    cos_a, sin_a = by_block[:, :quarter], by_block[:, quarter:]
    cos_b, sin_b = by_row[:, :quarter], by_row[:, quarter:]
    cosine = cos_a * cos_b - sin_a * sin_b
    sine = sin_a * cos_b + cos_a * sin_b

    cross.wait_recv()
    latent = part[rows_of(0, 0), :] + crossed[...]
    compressed = latent[:, :LATENT]
    variance = jnp.mean(compressed * compressed, axis=1, keepdims=True)
    normed = compressed * lax.rsqrt(variance + 1e-06) * gain_v[...]
    front, back = latent[:, LATENT : LATENT + quarter], latent[:, LATENT + quarter :]
    rotated = jnp.concatenate([front * cosine - back * sine, back * cosine + front * sine], 1)

    def piece(of_head):
        return keys.at[of_head // 8, SLOT[8], pl.ds(pl.multiple_of(of_head % 8 * ROWS, ROWS), ROWS), :]

    keys[head // 8, SLOT[8], pl.ds(pl.multiple_of(head % 8 * ROWS, ROWS), ROWS), :] = jnp.concatenate(
        [normed, rotated], 1
    ).astype(jnp.bfloat16)

    ag = []
    for i, (dz, dx) in enumerate(OFFSETS):
        copy = pltpu.make_async_remote_copy(
            src_ref=piece(head),
            dst_ref=piece(head),
            send_sem=ag_send.at[i],
            recv_sem=ag_recv.at[head],
            device_id=(ctx, head_peer(dz, dx)),
            device_id_type=MESH,
        )
        copy.start()
        ag.append(copy)

    def gathered(half, part_index):
        for i in range(CHUNK // ROWS):
            of_head = half * 8 + part_index * (CHUNK // ROWS) + i

            @pl.when(head != of_head)
            def _():
                pltpu.make_async_remote_copy(
                    src_ref=piece(of_head),
                    dst_ref=piece(of_head),
                    send_sem=ag_send.at[0],
                    recv_sem=ag_recv.at[of_head],
                    device_id=(ctx, head_peer(1, 0)),
                    device_id_type=MESH,
                ).wait_recv()

    sent = []

    def chunk(half, index, u):
        return keys.at[half, index, pl.ds(u * CHUNK, CHUNK), :]

    def either(bit, index, other):
        return SLOT[index] * (1 - bit) + SLOT[other] * bit

    def send(condition, half, index, u, to_half, to_index, to_ctx, to_head):
        copy = pltpu.make_async_remote_copy(
            src_ref=chunk(half, index, u),
            dst_ref=chunk(to_half, to_index, u),
            send_sem=win_send.at[len(sent)],
            recv_sem=win_recv.at[to_half, to_index, u],
            device_id=(to_ctx, to_head),
            device_id_type=MESH,
        )
        sent.append((condition, copy))
        if condition is None:
            copy.start()
        else:
            pl.when(condition)(copy.start)

    def take(half, index, u):
        pltpu.make_async_remote_copy(
            src_ref=chunk(half, index, u),
            dst_ref=chunk(half, index, u),
            send_sem=win_send.at[0],
            recv_sem=win_recv.at[half, index, u],
            device_id=(mate_ctx, head),
            device_id_type=MESH,
        ).wait_recv()

    place = {slot: index for index, slot in SLOT.items()}

    def score(first, count):
        for half in range(2):
            block_keys = keys[half, first : first + count].reshape(count * BLOCK, KEY)
            raw = lax.dot_general(
                qfull[half], block_keys, (((1,), (1,)), ((), ())), preferred_element_type=jnp.float32
            )
            highest = None if first == 0 else rowmax[half]
            for i in range(count):
                index = place[first + i]
                seen = index * BLOCK + lane >= lower[half]
                if index == SPAN - 1:
                    seen = seen & (lane <= row)
                own = raw[:, i * BLOCK : (i + 1) * BLOCK].reshape(heads, BLOCK, BLOCK)
                masked = jnp.where(seen[None], own, NEG).reshape(heads * BLOCK, BLOCK)
                scores[half, first + i] = masked
                highest = masked if highest is None else jnp.maximum(highest, masked)
            rowmax[half] = highest

    to_log2 = (NOPE + ROPE) ** -0.5 * 1.4426950408889634

    def weigh(half, first, count, top, total):
        for slot in range(first, first + count):
            weight = jnp.exp2((scores[half, slot] - top) * to_log2).astype(jnp.bfloat16)
            probs[:, slot * BLOCK : (slot + 1) * BLOCK] = weight
            total = total + weight.astype(jnp.float32)
        values = keys[half, first : first + count].reshape(count * BLOCK, KEY)[:, :LATENT]
        return total, jnp.dot(
            probs[:, first * BLOCK : (first + count) * BLOCK], values, preferred_element_type=jnp.float32
        )

    onward = y > 0
    for u in range(PARTS):
        gathered(0, u)
        send(None, 0, SLOT[8], u, last, SLOT[4], next_ctx, next_head)
        send(x_lo == 0, 0, SLOT[8], u, 0, SLOT[6], across_ctx, down_head)
        send(core == 0, 0, SLOT[8], u, 0, SLOT[7], mate_ctx, head)
    for u in range(PARTS):
        gathered(1, u)
        send(onward, 1, SLOT[8], u, 1, SLOT[4], ctx - 4, head)
        send(x_lo == 1, 1, SLOT[8], u, 1, SLOT[6], across_ctx, down_head)
        send(core == 1, 1, SLOT[8], u, 1, SLOT[7], mate_ctx, head)
    score(SLOT[8], 1)

    for u in range(PARTS):
        pl.when(onward)(functools.partial(take, 0, SLOT[4], u))
        send(None, 0, SLOT[4], u, last, SLOT[0], next_ctx, next_head)
        send(None, 0, SLOT[4], u, 0, either(x_lo, 2, 6), across_ctx, down_head)
        send(None, 0, SLOT[4], u, 0, either(core, 3, 5), mate_ctx, head)
        take(1, SLOT[4], u)
        send(onward, 1, SLOT[4], u, 1, SLOT[0], ctx - 4, head)
        send(None, 1, SLOT[4], u, 1, either(x_lo, 6, 2), across_ctx, down_head)
        send(None, 1, SLOT[4], u, 1, either(core, 5, 3), mate_ctx, head)
    score(SLOT[4], 1)

    for u in range(PARTS):
        pl.when(onward)(functools.partial(take, 0, SLOT[0], u))
        send(x_lo == 1, 0, SLOT[0], u, 0, SLOT[2], across_ctx, down_head)
        send(core == 1, 0, SLOT[0], u, 0, SLOT[1], mate_ctx, head)
        take(1, SLOT[0], u)
        send(x_lo == 0, 1, SLOT[0], u, 1, SLOT[2], across_ctx, down_head)
        send(core == 0, 1, SLOT[0], u, 1, SLOT[1], mate_ctx, head)
    for u in range(PARTS):
        for half in range(2):
            take(half, SLOT[6], u)
            to = either(core, 5, 7) if half == 0 else either(core, 7, 5)
            send(None, half, SLOT[6], u, half, to, mate_ctx, head)
    score(SLOT[0], 2)
    for half in range(2):
        top = jnp.max(rowmax[half], axis=1, keepdims=True)
        top_early[half] = jnp.broadcast_to(top, (heads * BLOCK, BLOCK))
        total_early[half], mixing[half] = weigh(
            half, 0, EARLY, top, jnp.zeros((heads * BLOCK, BLOCK), jnp.float32)
        )

    for u in range(PARTS):
        for half in range(2):
            take(half, SLOT[2], u)
            to = either(core, 1, 3) if half == 0 else either(core, 3, 1)
            send(None, half, SLOT[2], u, half, to, mate_ctx, head)
    for index in (7, 5):
        for half in range(2):
            for u in range(PARTS):
                take(half, SLOT[index], u)
    score(SLOT[2], 3)
    for index in (1, 3):
        for half in range(2):
            for u in range(PARTS):
                take(half, SLOT[index], u)
    score(SLOT[1], 2)

    loads[4].wait()
    for half in range(2):
        top = jnp.max(rowmax[half], axis=1, keepdims=True)
        fade = jnp.exp2((top_early[half] - top) * to_log2)
        total, numerator = weigh(half, EARLY, SPAN - EARLY, top, total_early[half] * fade)
        numerator = numerator + mixing[half] * fade[:, :1]
        mixed = (numerator * (1.0 / jnp.sum(total, axis=1, keepdims=True))).astype(jnp.bfloat16)
        for n in range(heads):
            out_ref[half, :, n * VDIM : (n + 1) * VDIM] = jnp.dot(
                mixed[n * BLOCK : (n + 1) * BLOCK], w_val_v[n], preferred_element_type=jnp.float32
            ).astype(jnp.bfloat16)

    for copy in [*rs.values(), *straight, cross, *ag]:
        copy.wait_send()
    for condition, copy in sent:
        if condition is None:
            copy.wait_send()
        else:
            pl.when(condition)(copy.wait_send)


def turns(positions):
    angles = positions[:, None] * 10000.0 ** (-np.arange(ROPE // 2) / (ROPE // 2))[None, :]
    return np.concatenate([np.cos(angles), np.sin(angles)], 1).astype(np.float32)


def on_device(hidden, queries, w_dkv, kv_gain, w_key, w_val, doc_lengths):
    heads = w_key.shape[0]
    hidden = jnp.swapaxes(hidden, 1, 2)
    turn_block = jnp.asarray(turns(np.arange(64) * BLOCK))
    turn_row = jnp.asarray(turns(np.arange(BLOCK)))
    any_space = pl.BlockSpec(memory_space=pl.ANY)
    in_vmem = pl.BlockSpec(memory_space=pltpu.VMEM)
    bf16, f32 = jnp.bfloat16, jnp.float32
    dma = pltpu.SemaphoreType.DMA
    return pl.pallas_call(
        body,
        out_shape=jax.ShapeDtypeStruct((2, BLOCK, heads * VDIM), bf16),
        in_specs=[any_space] * 9,
        out_specs=in_vmem,
        scratch_shapes=[
            pltpu.VMEM(hidden.shape, bf16),
            pltpu.VMEM(queries.shape, bf16),
            pltpu.VMEM(w_dkv.shape, bf16),
            pltpu.VMEM((1, LATENT), f32),
            pltpu.VMEM(w_key.shape, bf16),
            pltpu.VMEM(w_val.shape, bf16),
            pltpu.SMEM(doc_lengths.shape, jnp.int32),
            pltpu.VMEM(turn_block.shape, f32),
            pltpu.VMEM(turn_row.shape, f32),
            pltpu.VMEM((2 * BLOCK, KEY), f32),
            pltpu.VMEM((2 * REACH, ROWS, KEY), f32),
            pltpu.VMEM((2 * REACH, ROWS, KEY), f32),
            pltpu.VMEM((2, ROWS, KEY), f32),
            pltpu.VMEM((ROWS, KEY), f32),
            pltpu.VMEM((2, SPAN, BLOCK, KEY), bf16),
            pltpu.VMEM((2, heads * BLOCK, KEY), bf16),
            pltpu.VMEM((2, SPAN, heads * BLOCK, BLOCK), f32),
            pltpu.VMEM((2, heads * BLOCK, BLOCK), f32),
            pltpu.VMEM((2, BLOCK, BLOCK), jnp.int32),
            pltpu.VMEM((heads * BLOCK, SPAN * BLOCK), bf16),
            pltpu.VMEM((2, heads * BLOCK, BLOCK), f32),
            pltpu.VMEM((2, heads * BLOCK, BLOCK), f32),
            pltpu.VMEM((2, heads * BLOCK, LATENT), f32),
            dma((9,)), dma((2 * REACH,)), dma((2 * REACH,)), dma((2 * REACH,)), dma((2 * REACH,)), dma((2,)), dma((2,)), dma((2,)),
            dma((PEERS,)), dma((PEERS + 1,)), dma((40,)), dma((2, SPAN, PARTS)),
        ],
        compiler_params=pltpu.CompilerParams(
            collective_id=0, has_side_effects=True, vmem_limit_bytes=60 * 1024 * 1024
        ),
    )(hidden, queries, w_dkv, kv_gain.reshape(1, LATENT), w_key, w_val, doc_lengths, turn_block, turn_row)


def solution(mesh):
    in_specs = (
        P(None, "ctx", "head"),
        P(None, "ctx", "head"),
        P("head", None),
        P(),
        P("head", None, None),
        P("head", None, None),
        P(),
    )
    out_specs = P(None, "ctx", "head")
    return jax.shard_map(
        on_device, mesh=mesh, in_specs=in_specs, out_specs=out_specs, check_vma=False
    )
```

```python
import functools

import jax
import jax.numpy as jnp
import numpy as np
from jax import lax
from jax.experimental import pallas as pl
from jax.experimental.pallas import tpu as pltpu
from jax.sharding import PartitionSpec as P

LATENT = 512
ROPE = 64
NOPE = 128
VDIM = 128
KEY = LATENT + ROPE
WINDOW = 1024
SPAN = 9
BLOCK = 128
ROWS = 16
CHUNK = 64
PARTS = BLOCK // CHUNK
SLOT = {8: 0, 4: 1, 0: 2, 6: 3, 2: 4, 7: 5, 5: 6, 1: 7, 3: 8}
EARLY = 4
NEG = -1e30
MESH = pl.DeviceIdType.MESH

NEAR = [(dz, dx) for dz in (2, -2, 1, -1, 0) for dx in (1, 0) if (dz, dx) != (0, 0)]
PEERS = 15
ALONG = (4, 3, -3, 2, -2, 1, -1, 0)


def body(
    hidden_hbm, queries_hbm, w_dkv_hbm, gain_hbm, w_key_hbm, w_val_hbm, docs_hbm, turn_block_hbm, turn_row_hbm,
    out_ref,
    hidden_v, queries_v, w_dkv_v, gain_v, w_key_v, w_val_v, docs_s, turn_block_v, turn_row_v,
    part, crossed, arrived, keys, qfull, scores, rowmax, lower, probs, top_early, total_early, mixing,
    load_sem, cross_send, cross_recv, rs_send, rs_recv, ag_send, ag_recv, win_send, win_recv,
):
    ctx = lax.axis_index("ctx")
    head = lax.axis_index("head")
    core = ctx % 2
    x_lo = (ctx // 2) % 2
    y = ctx // 4
    col = ctx % 4
    z = head // 2
    x_hi = head % 2
    heads = w_key_v.shape[0]

    def head_peer(dz, dx):
        return ((z + dz + 8) % 8) * 2 + (x_hi + dx) % 2

    same = (x_lo + core + 1) % 2
    down_head = z * 2 + (x_hi + same) % 2
    up_head = z * 2 + (x_hi + 1 - same) % 2
    across_ctx = 4 * y + 2 * (1 - x_lo) + core
    mate_ctx = 4 * y + 2 * x_lo + 1 - core
    mirror_ctx = 4 * y + 3 - col
    last = y // 7
    next_ctx = (1 - last) * (ctx + 4) + last * mirror_ctx
    next_head = (1 - last) * head + last * down_head

    barrier = pltpu.get_barrier_semaphore()

    def greet(to_ctx, to_head):
        pl.semaphore_signal(barrier, inc=1, device_id=(to_ctx, to_head), device_id_type=MESH)

    greet(ctx, head_peer(0, 1))
    for dz in ALONG[:-1]:
        greet(ctx, head_peer(dz, 0))
    greet(across_ctx, down_head)
    greet(across_ctx, up_head)
    greet((ctx + 4) % 32, head)
    greet((ctx + 28) % 32, head)
    greet(mirror_ctx, down_head)
    greet(mate_ctx, head)

    loads = [
        pltpu.make_async_copy(source, target, load_sem.at[i])
        for i, (source, target) in enumerate(
            [
                (hidden_hbm, hidden_v),
                (w_dkv_hbm, w_dkv_v),
                (queries_hbm, queries_v),
                (w_key_hbm, w_key_v),
                (w_val_hbm, w_val_v),
                (docs_hbm, docs_s),
                (gain_hbm, gain_v),
                (turn_block_hbm, turn_block_v),
                (turn_row_hbm, turn_row_v),
            ]
        )
    ]
    loads[0].start()
    loads[1].start()
    loads[0].wait()
    loads[1].wait()
    for load in loads[2:]:
        load.start()
    for half in range(2):
        part[half * BLOCK : (half + 1) * BLOCK, :] = lax.dot_general(
            hidden_v[half], w_dkv_v[...], (((0,), (0,)), ((), ())), preferred_element_type=jnp.float32
        )

    pl.semaphore_wait(barrier, len(ALONG) + 6)

    def rows_of(dz, dx):
        return pl.ds(pl.multiple_of(head_peer(dz, dx) * ROWS, ROWS), ROWS)

    cross = []
    for i, dz in enumerate(ALONG):
        copy = pltpu.make_async_remote_copy(
            src_ref=part.at[rows_of(dz, 1), :],
            dst_ref=crossed.at[i],
            send_sem=cross_send.at[i],
            recv_sem=cross_recv.at[i],
            device_id=(ctx, head_peer(0, 1)),
            device_id_type=MESH,
        )
        copy.start()
        cross.append(copy)

    row = lax.broadcasted_iota(jnp.int32, (BLOCK, BLOCK), 0)
    lane = lax.broadcasted_iota(jnp.int32, (BLOCK, BLOCK), 1)

    def bounds():
        loads[5].wait()
        for half in range(2):
            query_block = ctx if half == 0 else 63 - ctx
            position = query_block * BLOCK + row
            start = jnp.zeros((BLOCK, BLOCK), jnp.int32)
            bound = jnp.int32(0)
            for i in range(docs_s.shape[0]):
                bound = bound + docs_s[i]
                start = jnp.maximum(start, jnp.where(bound <= position, bound, 0))
            lower[half] = jnp.maximum(start - (query_block - (SPAN - 1)) * BLOCK, row + 1)

    def absorb(half):
        for n in range(heads):
            at = n * (NOPE + ROPE)
            rows = slice(n * BLOCK, (n + 1) * BLOCK)
            qfull[half, rows, :LATENT] = lax.dot_general(
                queries_v[half, :, at : at + NOPE],
                w_key_v[n],
                (((1,), (1,)), ((), ())),
                preferred_element_type=jnp.float32,
            ).astype(jnp.bfloat16)
            qfull[half, rows, LATENT:] = queries_v[half, :, at + NOPE : at + NOPE + ROPE]

    @pl.when(y == 0)
    def _():
        keys[0, SLOT[0]] = jnp.zeros((BLOCK, KEY), jnp.bfloat16)
        keys[0, SLOT[4]] = jnp.zeros((BLOCK, KEY), jnp.bfloat16)

    bounds()
    rs = []
    for i, dz in enumerate(ALONG):
        cross[i].wait_recv()
        rows = rows_of(dz, 0)
        part[rows, :] = part[rows, :] + crossed[i]
        if dz != 0:
            copy = pltpu.make_async_remote_copy(
                src_ref=part.at[rows, :],
                dst_ref=arrived.at[i],
                send_sem=rs_send.at[i],
                recv_sem=rs_recv.at[i],
                device_id=(ctx, head_peer(dz, 0)),
                device_id_type=MESH,
            )
            copy.start()
            rs.append(copy)
    for i in (6, 7, 8):
        loads[i].wait()
    key_block = (1 - head // 8) * ctx + head // 8 * (63 - ctx)
    by_block = turn_block_v[pl.ds(key_block, 1), :]
    by_row = turn_row_v[pl.ds(pl.multiple_of(head % 8 * ROWS, ROWS), ROWS), :]
    quarter = ROPE // 2
    cos_a, sin_a = by_block[:, :quarter], by_block[:, quarter:]
    cos_b, sin_b = by_row[:, :quarter], by_row[:, quarter:]
    cosine = cos_a * cos_b - sin_a * sin_b
    sine = sin_a * cos_b + cos_a * sin_b

    latent = part[rows_of(0, 0), :]
    for i, copy in enumerate(rs):
        copy.wait_recv()
        latent = latent + arrived[i]
    compressed = latent[:, :LATENT]
    variance = jnp.mean(compressed * compressed, axis=1, keepdims=True)
    normed = compressed * lax.rsqrt(variance + 1e-06) * gain_v[...]
    front, back = latent[:, LATENT : LATENT + quarter], latent[:, LATENT + quarter :]
    rotated = jnp.concatenate([front * cosine - back * sine, back * cosine + front * sine], 1)

    def piece(of_head):
        return keys.at[of_head // 8, SLOT[8], pl.ds(pl.multiple_of(of_head % 8 * ROWS, ROWS), ROWS), :]

    keys[head // 8, SLOT[8], pl.ds(pl.multiple_of(head % 8 * ROWS, ROWS), ROWS), :] = jnp.concatenate(
        [normed, rotated], 1
    ).astype(jnp.bfloat16)

    ag = []

    def spread(of_head, to_head):
        copy = pltpu.make_async_remote_copy(
            src_ref=piece(of_head),
            dst_ref=piece(of_head),
            send_sem=ag_send.at[len(ag)],
            recv_sem=ag_recv.at[of_head],
            device_id=(ctx, to_head),
            device_id_type=MESH,
        )
        copy.start()
        ag.append(copy)

    def got(dz, dx):
        of_head = head_peer(dz, dx)
        pltpu.make_async_remote_copy(
            src_ref=piece(of_head),
            dst_ref=piece(of_head),
            send_sem=ag_send.at[0],
            recv_sem=ag_recv.at[of_head],
            device_id=(ctx, head_peer(1, 0)),
            device_id_type=MESH,
        ).wait_recv()

    for dz, dx in NEAR:
        spread(head, head_peer(dz, dx))

    loads[2].wait()
    loads[3].wait()
    absorb(0)
    absorb(1)

    sent = []

    def chunk(half, index, u):
        return keys.at[half, index, pl.ds(u * CHUNK, CHUNK), :]

    def either(bit, index, other):
        return SLOT[index] * (1 - bit) + SLOT[other] * bit

    def send(condition, half, index, u, to_half, to_index, to_ctx, to_head):
        copy = pltpu.make_async_remote_copy(
            src_ref=chunk(half, index, u),
            dst_ref=chunk(to_half, to_index, u),
            send_sem=win_send.at[len(sent)],
            recv_sem=win_recv.at[to_half, to_index, u],
            device_id=(to_ctx, to_head),
            device_id_type=MESH,
        )
        sent.append((condition, copy))
        if condition is None:
            copy.start()
        else:
            pl.when(condition)(copy.start)

    def take(half, index, u):
        pltpu.make_async_remote_copy(
            src_ref=chunk(half, index, u),
            dst_ref=chunk(half, index, u),
            send_sem=win_send.at[0],
            recv_sem=win_recv.at[half, index, u],
            device_id=(mate_ctx, head),
            device_id_type=MESH,
        ).wait_recv()

    place = {slot: index for index, slot in SLOT.items()}

    def score(first, count):
        for half in range(2):
            block_keys = keys[half, first : first + count].reshape(count * BLOCK, KEY)
            raw = lax.dot_general(
                qfull[half], block_keys, (((1,), (1,)), ((), ())), preferred_element_type=jnp.float32
            )
            highest = None if first == 0 else rowmax[half]
            for i in range(count):
                index = place[first + i]
                seen = index * BLOCK + lane >= lower[half]
                if index == SPAN - 1:
                    seen = seen & (lane <= row)
                own = raw[:, i * BLOCK : (i + 1) * BLOCK].reshape(heads, BLOCK, BLOCK)
                masked = jnp.where(seen[None], own, NEG).reshape(heads * BLOCK, BLOCK)
                scores[half, first + i] = masked
                highest = masked if highest is None else jnp.maximum(highest, masked)
            rowmax[half] = highest

    to_log2 = (NOPE + ROPE) ** -0.5 * 1.4426950408889634

    def weigh(half, first, count, top, total):
        for slot in range(first, first + count):
            weight = jnp.exp2((scores[half, slot] - top) * to_log2).astype(jnp.bfloat16)
            probs[:, slot * BLOCK : (slot + 1) * BLOCK] = weight
            total = total + weight.astype(jnp.float32)
        values = keys[half, first : first + count].reshape(count * BLOCK, KEY)[:, :LATENT]
        return total, jnp.dot(
            probs[:, first * BLOCK : (first + count) * BLOCK], values, preferred_element_type=jnp.float32
        )

    onward = y > 0
    toward = 1 - 2 * (z % 2)

    def pair(steps):
        which = (z // 2 + steps + 4) % 4
        return which // 2, which % 2

    own_pair, near_pair, middle_pair, far_pair = pair(0), pair(-toward), pair(toward), pair(2)

    def along_y(half, slot, u, to_slot):
        send(
            (half == 0) | onward,
            half, slot, u,
            half + (1 - half) * last, to_slot,
            (1 - half) * next_ctx + half * (ctx - 4), (1 - half) * next_head + half * head,
        )

    def unturned(half):
        return (half == 0) | (last == 0)

    def begin(half, u):
        along_y(half, SLOT[8], u, SLOT[4])
        send(x_lo == half, half, SLOT[8], u, half, SLOT[6], across_ctx, down_head)
        send(core == half, half, SLOT[8], u, half, SLOT[7], mate_ctx, head)
        send((half == 0) & (last == 1), half, SLOT[8], u, 1, either(x_lo, 2, 6), mate_ctx, head)

    def second(half, u):
        pl.when((half == 1) | onward)(functools.partial(take, half, SLOT[4], u))
        along_y(half, SLOT[4], u, SLOT[0])
        send(unturned(half), half, SLOT[4], u, half, either((x_lo + half) % 2, 2, 6), across_ctx, down_head)
        send(None, half, SLOT[4], u, half, either((core + half) % 2, 3, 5), mate_ctx, head)
        send((half == 0) & (last == 1) & (x_lo == 1), half, SLOT[4], u, 1, SLOT[2], mate_ctx, head)

    def third(half, u):
        pl.when((half == 1) | onward)(functools.partial(take, half, SLOT[0], u))
        send((x_lo != half) & unturned(half), half, SLOT[0], u, half, SLOT[2], across_ctx, down_head)
        send(core != half, half, SLOT[0], u, half, SLOT[1], mate_ctx, head)

    def across(half, u, slot, first, other):
        take(half, slot, u)
        send(None, half, slot, u, half, either((core + half) % 2, first, other), mate_ctx, head)

    got(0, 1)
    for dx in (0, 1):
        got(toward, dx)
    begin(*own_pair)
    for dz in (-2, 2):
        for plane in (0, 1):
            of_head = (z + dz + 8) % 8 * 2 + plane
            got(dz, (x_hi + plane) % 2)
            spread(of_head, head_peer(-dz // 2, 0))
            if dz == (-2 if plane == 0 else 2):
                spread(of_head, head_peer(-dz, 0))
    for dx in (0, 1):
        got(-toward, dx)
    begin(*near_pair)
    for dx in (0, 1):
        got(3 * toward, dx)
    begin(*middle_pair)
    for dx in (0, 1):
        got(4, dx)
        got(-3 * toward, dx)
    begin(*far_pair)
    order = (own_pair, near_pair, middle_pair, far_pair)
    second(*order[0])
    second(*order[1])
    score(SLOT[8], 1)
    second(*order[2])
    second(*order[3])
    for which in order:
        third(*which)
    for which in order:
        across(*which, SLOT[6], 5, 7)
    score(SLOT[4], 3)
    for half in range(2):
        top = jnp.max(rowmax[half], axis=1, keepdims=True)
        top_early[half] = jnp.broadcast_to(top, (heads * BLOCK, BLOCK))
        total_early[half], mixing[half] = weigh(
            half, 0, EARLY, top, jnp.zeros((heads * BLOCK, BLOCK), jnp.float32)
        )
    for which in order:
        across(*which, SLOT[2], 1, 3)
    for index in (7, 5):
        for half in range(2):
            for u in range(PARTS):
                take(half, SLOT[index], u)
    score(SLOT[2], 3)
    for index in (1, 3):
        for half in range(2):
            for u in range(PARTS):
                take(half, SLOT[index], u)
    score(SLOT[1], 2)

    loads[4].wait()
    for half in range(2):
        top = jnp.max(rowmax[half], axis=1, keepdims=True)
        fade = jnp.exp2((top_early[half] - top) * to_log2)
        total, numerator = weigh(half, EARLY, SPAN - EARLY, top, total_early[half] * fade)
        numerator = numerator + mixing[half] * fade[:, :1]
        mixed = (numerator * (1.0 / jnp.sum(total, axis=1, keepdims=True))).astype(jnp.bfloat16)
        for n in range(heads):
            out_ref[half, :, n * VDIM : (n + 1) * VDIM] = jnp.dot(
                mixed[n * BLOCK : (n + 1) * BLOCK], w_val_v[n], preferred_element_type=jnp.float32
            ).astype(jnp.bfloat16)

    for copy in [*cross, *rs, *ag]:
        copy.wait_send()
    for condition, copy in sent:
        if condition is None:
            copy.wait_send()
        else:
            pl.when(condition)(copy.wait_send)


def turns(positions):
    angles = positions[:, None] * 10000.0 ** (-np.arange(ROPE // 2) / (ROPE // 2))[None, :]
    return np.concatenate([np.cos(angles), np.sin(angles)], 1).astype(np.float32)


def on_device(hidden, queries, w_dkv, kv_gain, w_key, w_val, doc_lengths):
    heads = w_key.shape[0]
    hidden = jnp.swapaxes(hidden, 1, 2)
    turn_block = jnp.asarray(turns(np.arange(64) * BLOCK))
    turn_row = jnp.asarray(turns(np.arange(BLOCK)))
    any_space = pl.BlockSpec(memory_space=pl.ANY)
    in_vmem = pl.BlockSpec(memory_space=pltpu.VMEM)
    bf16, f32 = jnp.bfloat16, jnp.float32
    dma = pltpu.SemaphoreType.DMA
    return pl.pallas_call(
        body,
        out_shape=jax.ShapeDtypeStruct((2, BLOCK, heads * VDIM), bf16),
        in_specs=[any_space] * 9,
        out_specs=in_vmem,
        scratch_shapes=[
            pltpu.VMEM(hidden.shape, bf16),
            pltpu.VMEM(queries.shape, bf16),
            pltpu.VMEM(w_dkv.shape, bf16),
            pltpu.VMEM((1, LATENT), f32),
            pltpu.VMEM(w_key.shape, bf16),
            pltpu.VMEM(w_val.shape, bf16),
            pltpu.SMEM(doc_lengths.shape, jnp.int32),
            pltpu.VMEM(turn_block.shape, f32),
            pltpu.VMEM(turn_row.shape, f32),
            pltpu.VMEM((2 * BLOCK, KEY), f32),
            pltpu.VMEM((len(ALONG), ROWS, KEY), f32),
            pltpu.VMEM((len(ALONG) - 1, ROWS, KEY), f32),
            pltpu.VMEM((2, SPAN, BLOCK, KEY), bf16),
            pltpu.VMEM((2, heads * BLOCK, KEY), bf16),
            pltpu.VMEM((2, SPAN, heads * BLOCK, BLOCK), f32),
            pltpu.VMEM((2, heads * BLOCK, BLOCK), f32),
            pltpu.VMEM((2, BLOCK, BLOCK), jnp.int32),
            pltpu.VMEM((heads * BLOCK, SPAN * BLOCK), bf16),
            pltpu.VMEM((2, heads * BLOCK, BLOCK), f32),
            pltpu.VMEM((2, heads * BLOCK, BLOCK), f32),
            pltpu.VMEM((2, heads * BLOCK, LATENT), f32),
            dma((9,)), dma((8,)), dma((8,)), dma((7,)), dma((7,)),
            dma((PEERS,)), dma((PEERS + 1,)), dma((48,)), dma((2, SPAN, PARTS)),
        ],
        compiler_params=pltpu.CompilerParams(
            collective_id=0, has_side_effects=True, vmem_limit_bytes=60 * 1024 * 1024
        ),
    )(hidden, queries, w_dkv, kv_gain.reshape(1, LATENT), w_key, w_val, doc_lengths, turn_block, turn_row)


def solution(mesh):
    in_specs = (
        P(None, "ctx", "head"),
        P(None, "ctx", "head"),
        P("head", None),
        P(),
        P("head", None, None),
        P("head", None, None),
        P(),
    )
    out_specs = P(None, "ctx", "head")
    return jax.shard_map(
        on_device, mesh=mesh, in_specs=in_specs, out_specs=out_specs, check_vma=False
    )
```

```python
import functools

import jax
import jax.numpy as jnp
import numpy as np
from jax import lax
from jax.experimental import pallas as pl
from jax.experimental.pallas import tpu as pltpu
from jax.sharding import PartitionSpec as P

LATENT = 512
ROPE = 64
NOPE = 128
VDIM = 128
KEY = LATENT + ROPE
WINDOW = 1024
SPAN = 9
BLOCK = 128
ROWS = 16
CHUNK = 64
PARTS = BLOCK // CHUNK
SLOT = {8: 0, 4: 1, 0: 2, 6: 3, 2: 4, 7: 5, 5: 6, 1: 7, 3: 8}
EARLY = 4
NEG = -1e30
MESH = pl.DeviceIdType.MESH

NEAR = [(dz, dx) for dz in (2, -2, 1, -1, 0) for dx in (1, 0) if (dz, dx) != (0, 0)]
PEERS = 15
ALONG = (4, 3, -3, 2, -2, 1, -1, 0)


def body(
    hidden_hbm, queries_hbm, w_dkv_hbm, gain_hbm, w_key_hbm, w_val_hbm, docs_hbm, turn_block_hbm, turn_row_hbm,
    out_hbm,
    hidden_v, queries_v, w_dkv_v, gain_v, w_key_v, w_val_v, docs_s, turn_block_v, turn_row_v,
    part, crossed, arrived, keys, qfull, scores, rowmax, lower, probs, top_early, total_early, mixing, result,
    out_sem,
    load_sem, cross_send, cross_recv, rs_send, rs_recv, ag_send, ag_recv, win_send, win_recv,
):
    ctx = lax.axis_index("ctx")
    head = lax.axis_index("head")
    core = ctx % 2
    x_lo = (ctx // 2) % 2
    y = ctx // 4
    col = ctx % 4
    z = head // 2
    x_hi = head % 2
    heads = w_key_v.shape[0]

    def head_peer(dz, dx):
        return ((z + dz + 8) % 8) * 2 + (x_hi + dx) % 2

    same = (x_lo + core + 1) % 2
    down_head = z * 2 + (x_hi + same) % 2
    up_head = z * 2 + (x_hi + 1 - same) % 2
    across_ctx = 4 * y + 2 * (1 - x_lo) + core
    mate_ctx = 4 * y + 2 * x_lo + 1 - core
    mirror_ctx = 4 * y + 3 - col
    last = y // 7
    next_ctx = (1 - last) * (ctx + 4) + last * mirror_ctx
    next_head = (1 - last) * head + last * down_head

    barrier = pltpu.get_barrier_semaphore()

    def greet(to_ctx, to_head):
        pl.semaphore_signal(barrier, inc=1, device_id=(to_ctx, to_head), device_id_type=MESH)

    greet(ctx, head_peer(0, 1))
    for dz in ALONG[:-1]:
        greet(ctx, head_peer(dz, 0))
    greet(across_ctx, down_head)
    greet(across_ctx, up_head)
    greet((ctx + 4) % 32, head)
    greet((ctx + 28) % 32, head)
    greet(mirror_ctx, down_head)
    greet(mate_ctx, head)

    loads = [
        pltpu.make_async_copy(source, target, load_sem.at[i])
        for i, (source, target) in enumerate(
            [
                (hidden_hbm, hidden_v),
                (w_dkv_hbm, w_dkv_v),
                (queries_hbm, queries_v),
                (w_key_hbm, w_key_v),
                (w_val_hbm, w_val_v),
                (docs_hbm, docs_s),
                (gain_hbm, gain_v),
                (turn_block_hbm, turn_block_v),
                (turn_row_hbm, turn_row_v),
            ]
        )
    ]
    loads[0].start()
    loads[1].start()
    loads[0].wait()
    loads[1].wait()
    for load in loads[2:]:
        load.start()
    for half in range(2):
        part[half * BLOCK : (half + 1) * BLOCK, :] = lax.dot_general(
            hidden_v[half], w_dkv_v[...], (((0,), (0,)), ((), ())), preferred_element_type=jnp.float32
        )

    pl.semaphore_wait(barrier, len(ALONG) + 6)

    def rows_of(dz, dx):
        return pl.ds(pl.multiple_of(head_peer(dz, dx) * ROWS, ROWS), ROWS)

    cross = []
    for i, dz in enumerate(ALONG):
        copy = pltpu.make_async_remote_copy(
            src_ref=part.at[rows_of(dz, 1), :],
            dst_ref=crossed.at[i],
            send_sem=cross_send.at[i],
            recv_sem=cross_recv.at[i],
            device_id=(ctx, head_peer(0, 1)),
            device_id_type=MESH,
        )
        copy.start()
        cross.append(copy)

    row = lax.broadcasted_iota(jnp.int32, (BLOCK, BLOCK), 0)
    lane = lax.broadcasted_iota(jnp.int32, (BLOCK, BLOCK), 1)

    def bounds():
        loads[5].wait()
        for half in range(2):
            query_block = ctx if half == 0 else 63 - ctx
            position = query_block * BLOCK + row
            start = jnp.zeros((BLOCK, BLOCK), jnp.int32)
            bound = jnp.int32(0)
            for i in range(docs_s.shape[0]):
                bound = bound + docs_s[i]
                start = jnp.maximum(start, jnp.where(bound <= position, bound, 0))
            lower[half] = jnp.maximum(start - (query_block - (SPAN - 1)) * BLOCK, row + 1)

    def absorb(half):
        for n in range(heads):
            at = n * (NOPE + ROPE)
            rows = slice(n * BLOCK, (n + 1) * BLOCK)
            qfull[half, rows, :LATENT] = lax.dot_general(
                queries_v[half, :, at : at + NOPE],
                w_key_v[n],
                (((1,), (1,)), ((), ())),
                preferred_element_type=jnp.float32,
            ).astype(jnp.bfloat16)
            qfull[half, rows, LATENT:] = queries_v[half, :, at + NOPE : at + NOPE + ROPE]

    @pl.when(y == 0)
    def _():
        keys[0, SLOT[0]] = jnp.zeros((BLOCK, KEY), jnp.bfloat16)
        keys[0, SLOT[4]] = jnp.zeros((BLOCK, KEY), jnp.bfloat16)

    bounds()
    rs = []
    for i, dz in enumerate(ALONG):
        cross[i].wait_recv()
        rows = rows_of(dz, 0)
        part[rows, :] = part[rows, :] + crossed[i]
        if dz != 0:
            copy = pltpu.make_async_remote_copy(
                src_ref=part.at[rows, :],
                dst_ref=arrived.at[i],
                send_sem=rs_send.at[i],
                recv_sem=rs_recv.at[i],
                device_id=(ctx, head_peer(dz, 0)),
                device_id_type=MESH,
            )
            copy.start()
            rs.append(copy)
    for i in (6, 7, 8):
        loads[i].wait()
    key_block = (1 - head // 8) * ctx + head // 8 * (63 - ctx)
    by_block = turn_block_v[pl.ds(key_block, 1), :]
    by_row = turn_row_v[pl.ds(pl.multiple_of(head % 8 * ROWS, ROWS), ROWS), :]
    quarter = ROPE // 2
    cos_a, sin_a = by_block[:, :quarter], by_block[:, quarter:]
    cos_b, sin_b = by_row[:, :quarter], by_row[:, quarter:]
    cosine = cos_a * cos_b - sin_a * sin_b
    sine = sin_a * cos_b + cos_a * sin_b

    latent = part[rows_of(0, 0), :]
    for i, copy in enumerate(rs):
        copy.wait_recv()
        latent = latent + arrived[i]
    compressed = latent[:, :LATENT]
    variance = jnp.mean(compressed * compressed, axis=1, keepdims=True)
    normed = compressed * lax.rsqrt(variance + 1e-06) * gain_v[...]
    front, back = latent[:, LATENT : LATENT + quarter], latent[:, LATENT + quarter :]
    rotated = jnp.concatenate([front * cosine - back * sine, back * cosine + front * sine], 1)

    def piece(of_head):
        return keys.at[of_head // 8, SLOT[8], pl.ds(pl.multiple_of(of_head % 8 * ROWS, ROWS), ROWS), :]

    keys[head // 8, SLOT[8], pl.ds(pl.multiple_of(head % 8 * ROWS, ROWS), ROWS), :] = jnp.concatenate(
        [normed, rotated], 1
    ).astype(jnp.bfloat16)

    ag = []

    def spread(of_head, to_head):
        copy = pltpu.make_async_remote_copy(
            src_ref=piece(of_head),
            dst_ref=piece(of_head),
            send_sem=ag_send.at[len(ag)],
            recv_sem=ag_recv.at[of_head],
            device_id=(ctx, to_head),
            device_id_type=MESH,
        )
        copy.start()
        ag.append(copy)

    def got(dz, dx):
        of_head = head_peer(dz, dx)
        pltpu.make_async_remote_copy(
            src_ref=piece(of_head),
            dst_ref=piece(of_head),
            send_sem=ag_send.at[0],
            recv_sem=ag_recv.at[of_head],
            device_id=(ctx, head_peer(1, 0)),
            device_id_type=MESH,
        ).wait_recv()

    for dz, dx in NEAR:
        spread(head, head_peer(dz, dx))

    loads[2].wait()
    loads[3].wait()
    absorb(0)
    absorb(1)

    sent = []

    def chunk(half, index, u):
        return keys.at[half, index, pl.ds(u * CHUNK, CHUNK), :]

    def either(bit, index, other):
        return SLOT[index] * (1 - bit) + SLOT[other] * bit

    def send(condition, half, index, u, to_half, to_index, to_ctx, to_head):
        copy = pltpu.make_async_remote_copy(
            src_ref=chunk(half, index, u),
            dst_ref=chunk(to_half, to_index, u),
            send_sem=win_send.at[len(sent)],
            recv_sem=win_recv.at[to_half, to_index, u],
            device_id=(to_ctx, to_head),
            device_id_type=MESH,
        )
        sent.append((condition, copy))
        if condition is None:
            copy.start()
        else:
            pl.when(condition)(copy.start)

    def take(half, index, u):
        pltpu.make_async_remote_copy(
            src_ref=chunk(half, index, u),
            dst_ref=chunk(half, index, u),
            send_sem=win_send.at[0],
            recv_sem=win_recv.at[half, index, u],
            device_id=(mate_ctx, head),
            device_id_type=MESH,
        ).wait_recv()

    place = {slot: index for index, slot in SLOT.items()}

    def score(first, count):
        for half in range(2):
            block_keys = keys[half, first : first + count].reshape(count * BLOCK, KEY)
            raw = lax.dot_general(
                qfull[half], block_keys, (((1,), (1,)), ((), ())), preferred_element_type=jnp.float32
            )
            highest = None if first == 0 else rowmax[half]
            for i in range(count):
                index = place[first + i]
                seen = index * BLOCK + lane >= lower[half]
                if index == SPAN - 1:
                    seen = seen & (lane <= row)
                own = raw[:, i * BLOCK : (i + 1) * BLOCK].reshape(heads, BLOCK, BLOCK)
                masked = jnp.where(seen[None], own, NEG).reshape(heads * BLOCK, BLOCK)
                scores[half, first + i] = masked
                highest = masked if highest is None else jnp.maximum(highest, masked)
            rowmax[half] = highest

    to_log2 = (NOPE + ROPE) ** -0.5 * 1.4426950408889634

    def weigh(half, first, count, top, total):
        for slot in range(first, first + count):
            weight = jnp.exp2((scores[half, slot] - top) * to_log2).astype(jnp.bfloat16)
            probs[:, slot * BLOCK : (slot + 1) * BLOCK] = weight
            total = total + weight.astype(jnp.float32)
        values = keys[half, first : first + count].reshape(count * BLOCK, KEY)[:, :LATENT]
        return total, jnp.dot(
            probs[:, first * BLOCK : (first + count) * BLOCK], values, preferred_element_type=jnp.float32
        )

    onward = y > 0
    toward = 1 - 2 * (z % 2)

    def pair(steps):
        which = (z // 2 + steps + 4) % 4
        return which // 2, which % 2

    own_pair, near_pair, middle_pair, far_pair = pair(0), pair(-toward), pair(toward), pair(2)

    def along_y(half, slot, u, to_slot):
        send(
            (half == 0) | onward,
            half, slot, u,
            half + (1 - half) * last, to_slot,
            (1 - half) * next_ctx + half * (ctx - 4), (1 - half) * next_head + half * head,
        )

    def unturned(half):
        return (half == 0) | (last == 0)

    def begin(half, u):
        along_y(half, SLOT[8], u, SLOT[4])
        send(x_lo == half, half, SLOT[8], u, half, SLOT[6], across_ctx, down_head)
        send(core == half, half, SLOT[8], u, half, SLOT[7], mate_ctx, head)
        send((half == 0) & (last == 1), half, SLOT[8], u, 1, either(x_lo, 2, 6), mate_ctx, head)

    def second(half, u):
        pl.when((half == 1) | onward)(functools.partial(take, half, SLOT[4], u))
        along_y(half, SLOT[4], u, SLOT[0])
        send(unturned(half), half, SLOT[4], u, half, either((x_lo + half) % 2, 2, 6), across_ctx, down_head)
        send(None, half, SLOT[4], u, half, either((core + half) % 2, 3, 5), mate_ctx, head)
        send((half == 0) & (last == 1) & (x_lo == 1), half, SLOT[4], u, 1, SLOT[2], mate_ctx, head)

    def third(half, u):
        pl.when((half == 1) | onward)(functools.partial(take, half, SLOT[0], u))
        send((x_lo != half) & unturned(half), half, SLOT[0], u, half, SLOT[2], across_ctx, down_head)
        send(core != half, half, SLOT[0], u, half, SLOT[1], mate_ctx, head)

    def across(half, u, slot, first, other):
        take(half, slot, u)
        send(None, half, slot, u, half, either((core + half) % 2, first, other), mate_ctx, head)

    got(0, 1)
    for dx in (0, 1):
        got(toward, dx)
    begin(*own_pair)
    for dz in (-2, 2):
        for plane in (0, 1):
            of_head = (z + dz + 8) % 8 * 2 + plane
            got(dz, (x_hi + plane) % 2)
            spread(of_head, head_peer(-dz // 2, 0))
            if dz == (-2 if plane == 0 else 2):
                spread(of_head, head_peer(-dz, 0))
    for dx in (0, 1):
        got(-toward, dx)
    begin(*near_pair)
    for dx in (0, 1):
        got(3 * toward, dx)
    begin(*middle_pair)
    for dx in (0, 1):
        got(4, dx)
        got(-3 * toward, dx)
    begin(*far_pair)
    order = (own_pair, near_pair, middle_pair, far_pair)
    second(*order[0])
    second(*order[1])
    score(SLOT[8], 1)
    second(*order[2])
    second(*order[3])
    third(*order[0])
    third(*order[1])
    across(*order[0], SLOT[6], 5, 7)
    across(*order[1], SLOT[6], 5, 7)
    score(SLOT[4], 1)
    third(*order[2])
    third(*order[3])
    across(*order[2], SLOT[6], 5, 7)
    across(*order[3], SLOT[6], 5, 7)
    across(*order[0], SLOT[2], 1, 3)
    across(*order[1], SLOT[2], 1, 3)
    score(SLOT[0], 2)
    for half in range(2):
        top = jnp.max(rowmax[half], axis=1, keepdims=True)
        top_early[half] = jnp.broadcast_to(top, (heads * BLOCK, BLOCK))
        total_early[half], mixing[half] = weigh(
            half, 0, EARLY, top, jnp.zeros((heads * BLOCK, BLOCK), jnp.float32)
        )
    across(*order[2], SLOT[2], 1, 3)
    across(*order[3], SLOT[2], 1, 3)
    for index in (7, 5):
        for half in range(2):
            for u in range(PARTS):
                take(half, SLOT[index], u)
    score(SLOT[2], 3)
    for index in (1, 3):
        for half in range(2):
            for u in range(PARTS):
                take(half, SLOT[index], u)
    score(SLOT[1], 2)

    loads[4].wait()
    outs = []
    for half in range(2):
        top = jnp.max(rowmax[half], axis=1, keepdims=True)
        fade = jnp.exp2((top_early[half] - top) * to_log2)
        total, numerator = weigh(half, EARLY, SPAN - EARLY, top, total_early[half] * fade)
        numerator = numerator + mixing[half] * fade[:, :1]
        mixed = (numerator * (1.0 / jnp.sum(total, axis=1, keepdims=True))).astype(jnp.bfloat16)
        for n in range(heads):
            result[half, :, n * VDIM : (n + 1) * VDIM] = jnp.dot(
                mixed[n * BLOCK : (n + 1) * BLOCK], w_val_v[n], preferred_element_type=jnp.float32
            ).astype(jnp.bfloat16)

        out_copy = pltpu.make_async_copy(result.at[half], out_hbm.at[half], out_sem.at[half])
        out_copy.start()
        outs.append(out_copy)

    for copy in outs:
        copy.wait()
    for copy in [*cross, *rs, *ag]:
        copy.wait_send()
    for condition, copy in sent:
        if condition is None:
            copy.wait_send()
        else:
            pl.when(condition)(copy.wait_send)


def turns(positions):
    angles = positions[:, None] * 10000.0 ** (-np.arange(ROPE // 2) / (ROPE // 2))[None, :]
    return np.concatenate([np.cos(angles), np.sin(angles)], 1).astype(np.float32)


def on_device(hidden, queries, w_dkv, kv_gain, w_key, w_val, doc_lengths):
    heads = w_key.shape[0]
    hidden = jnp.swapaxes(hidden, 1, 2)
    turn_block = jnp.asarray(turns(np.arange(64) * BLOCK))
    turn_row = jnp.asarray(turns(np.arange(BLOCK)))
    any_space = pl.BlockSpec(memory_space=pl.ANY)
    bf16, f32 = jnp.bfloat16, jnp.float32
    dma = pltpu.SemaphoreType.DMA
    return pl.pallas_call(
        body,
        out_shape=jax.ShapeDtypeStruct((2, BLOCK, heads * VDIM), bf16),
        in_specs=[any_space] * 9,
        out_specs=any_space,
        scratch_shapes=[
            pltpu.VMEM(hidden.shape, bf16),
            pltpu.VMEM(queries.shape, bf16),
            pltpu.VMEM(w_dkv.shape, bf16),
            pltpu.VMEM((1, LATENT), f32),
            pltpu.VMEM(w_key.shape, bf16),
            pltpu.VMEM(w_val.shape, bf16),
            pltpu.SMEM(doc_lengths.shape, jnp.int32),
            pltpu.VMEM(turn_block.shape, f32),
            pltpu.VMEM(turn_row.shape, f32),
            pltpu.VMEM((2 * BLOCK, KEY), f32),
            pltpu.VMEM((len(ALONG), ROWS, KEY), f32),
            pltpu.VMEM((len(ALONG) - 1, ROWS, KEY), f32),
            pltpu.VMEM((2, SPAN, BLOCK, KEY), bf16),
            pltpu.VMEM((2, heads * BLOCK, KEY), bf16),
            pltpu.VMEM((2, SPAN, heads * BLOCK, BLOCK), f32),
            pltpu.VMEM((2, heads * BLOCK, BLOCK), f32),
            pltpu.VMEM((2, BLOCK, BLOCK), jnp.int32),
            pltpu.VMEM((heads * BLOCK, SPAN * BLOCK), bf16),
            pltpu.VMEM((2, heads * BLOCK, BLOCK), f32),
            pltpu.VMEM((2, heads * BLOCK, BLOCK), f32),
            pltpu.VMEM((2, heads * BLOCK, LATENT), f32),
            pltpu.VMEM((2, BLOCK, heads * VDIM), bf16),
            dma((2,)),
            dma((9,)), dma((8,)), dma((8,)), dma((7,)), dma((7,)),
            dma((PEERS,)), dma((PEERS + 1,)), dma((48,)), dma((2, SPAN, PARTS)),
        ],
        compiler_params=pltpu.CompilerParams(
            collective_id=0, has_side_effects=True, vmem_limit_bytes=60 * 1024 * 1024
        ),
    )(hidden, queries, w_dkv, kv_gain.reshape(1, LATENT), w_key, w_val, doc_lengths, turn_block, turn_row)


def solution(mesh):
    in_specs = (
        P(None, "ctx", "head"),
        P(None, "ctx", "head"),
        P("head", None),
        P(),
        P("head", None, None),
        P("head", None, None),
        P(),
    )
    out_specs = P(None, "ctx", "head")
    return jax.shard_map(
        on_device, mesh=mesh, in_specs=in_specs, out_specs=out_specs, check_vma=False
    )
```
